32 devices in a mesh: mem: 16 (over z, x, core), space: 2 (over y).
Axes of the slice: x: 2, y: 2, z: 4, core: 2. Of those that a mesh axis runs over, the one named last changes fastest.
Arguments:
- prior_samples: bfloat16 [256, 32, 4096], P('mem', 'space'), may hold values from -6 to 6
- diffusivity_field: float32 [32, 4096], P('space'), may hold values from 0.05 to 0.24
- measured_site_position: int32 [2, 16, 512], P('space', 'mem'), may hold values from 0 to 4095
- measured_quantities: float32 [2, 16, 512], P('space', 'mem'), may hold values from -6 to 6
- measurement_weightings: float32 [2, 16, 512], P('space', 'mem'), may hold values from 0.5 to 8
Outputs:
- analysis: bfloat16 [256, 32, 4096], P('mem', 'space')
The draws below stay inside these ranges and needn't reach their ends.
Inputs may be any that keep to these rules, and one draw needn't show every extreme that they name: measured_site_position[p, q, o] names cell a * 256 + b of patch (p, q) itself.
All inputs are finite; a program needn't handle non-finite values.
Results may differ from the reference program's by a relative error of at most 0.0077.
Values may be sent and summed in bfloat16 or wider, within the bound.
A program may use at most 64 MiB of HBM per device.

```python
import math
import jax
import jax.numpy as jnp
from jax import lax

SAMPLE_TOTAL = 256
A_DEV = 16
B_DEV = 256
OBS_DEV = 512
ITERS = 10
BLOCKS_A = 2
BLOCKS_B = 16
MESH_HEIGHT = 32
MESH_WIDTH = 4096


def with_ends(result, own_key, smallest, high):
    spot = [jax.random.randint(jax.random.fold_in(own_key, axis), (), 0, length) for axis, length in enumerate(result.shape)]
    longest = result.shape.index(max(result.shape))
    next_to = spot[:longest] + [(spot[longest] + 1) % result.shape[longest]] + spot[longest + 1:]
    return result.at[tuple(spot)].set(smallest).at[tuple(next_to)].set(high)


def steps_of(rng, dims, cuts, low, high):
    level, own = 1.0, jax.random.fold_in(rng, 6)
    for dim, shards_of in cuts:
        draws = jnp.exp(jax.random.uniform(jax.random.fold_in(own, dim), (shards_of,), jnp.float32, low / len(cuts), high / len(cuts)))
        level = level * jnp.repeat(draws, dims[dim] // shards_of).reshape([-1 if axis == dim else 1 for axis in range(len(dims))])
    return level


def scatter_about(stream_key, shape, scale, limit, split=(), kind=jnp.bfloat16):
    drawn = jax.random.normal(stream_key, shape, jnp.float32) * scale
    if len(split) > 0:
        drawn = steps_of(stream_key, shape, split, -0.22, 0.18) * drawn
    return jnp.clip(drawn, min=-limit, max=limit).astype(kind)


def setup_inputs(seed: int = 0) -> dict:
    arg_keys = jax.random.split(jax.random.key(seed), 6)
    prior_samples = scatter_about(arg_keys[0], (SAMPLE_TOTAL, MESH_HEIGHT, MESH_WIDTH), 1.0, 6.0, ((0, 16), (1, 2)))
    diffusivity_field = jnp.clip(0.05 + 0.19 * jax.random.uniform(arg_keys[1], (MESH_HEIGHT, MESH_WIDTH), jnp.float32) ** steps_of(arg_keys[1], (MESH_HEIGHT, MESH_WIDTH), ((0, 2),), -0.2, 0.2), 0.05, 0.24)
    measured_site_position = with_ends(jax.random.randint(arg_keys[2], (BLOCKS_A, BLOCKS_B, OBS_DEV), 0, A_DEV * B_DEV), jax.random.fold_in(arg_keys[2], 1), 0, (A_DEV * B_DEV) - 1).astype(jnp.int32)
    measured_quantities = scatter_about(arg_keys[3], (BLOCKS_A, BLOCKS_B, OBS_DEV), 1.0, 6.0, ((0, 2), (1, 16)), jnp.float32)
    measurement_weightings = jnp.clip(jnp.exp(math.log(8.0) - 2.7725887 * jax.random.uniform(arg_keys[4], (BLOCKS_A, BLOCKS_B, OBS_DEV), jnp.float32) ** steps_of(arg_keys[4], (BLOCKS_A, BLOCKS_B, OBS_DEV), ((0, 2), (1, 16)), -0.2, 0.2)), 0.5, 8.0)
    return {"prior_samples": prior_samples, "diffusivity_field": diffusivity_field, "measured_site_position": measured_site_position, "measured_quantities": measured_quantities, "measurement_weightings": measurement_weightings}


LOCALITY = ((0.25, 0.5, 0.25), (0.5, 1.0, 0.5), (0.25, 0.5, 0.25))
HIGHEST = lax.Precision.HIGHEST

def laplace(grid):
    padded = jnp.pad(grid, ((1, 1), (1, 1)))
    return padded[2:, 1:-1] + padded[:-2, 1:-1] + padded[1:-1, 2:] + padded[1:-1, :-2] - 4.0 * grid

def advance_prior(sample_label, diffusivity_field):
    present_sample = sample_label.astype(jnp.float32)
    present_sample = present_sample + diffusivity_field * laplace(present_sample)
    present_sample = present_sample + diffusivity_field * laplace(present_sample)
    return present_sample.astype(jnp.bfloat16)

def finish(sample_label, diffusivity_field):
    present_sample = sample_label.astype(jnp.float32)
    return (present_sample + diffusivity_field * laplace(present_sample)).astype(jnp.bfloat16)

def observe(patch_cells, indices, values, obs_weight):
    observed = jnp.take(patch_cells, indices, axis=1).astype(jnp.float32)
    obs_mean = lax.optimization_barrier(jnp.mean(observed, axis=0))
    obs_root = jnp.sqrt(obs_weight)
    spread = ((observed - obs_mean[None, :]) * obs_root[None, :]).astype(jnp.bfloat16)
    innovation = ((values - obs_mean) * obs_root).astype(jnp.bfloat16)
    spread_full = spread.astype(jnp.float32)
    own_gram = jnp.dot(spread_full, spread_full.T, precision=HIGHEST)
    own_vector = jnp.dot(spread_full, innovation.astype(jnp.float32), precision=HIGHEST)
    return (own_gram, own_vector)

def analyse(patch_cells, gram, vector):
    identity = jnp.eye(SAMPLE_TOTAL, dtype=jnp.float32)
    system = gram + (SAMPLE_TOTAL - 1.0) * identity
    frobenius = jnp.sqrt(jnp.sum(system * system))

    def newton(counter, pair):
        root_part, inverse_part = pair
        factor = 1.5 * identity - 0.5 * jnp.dot(inverse_part, root_part, precision=HIGHEST)
        return (jnp.dot(root_part, factor, precision=HIGHEST), jnp.dot(factor, inverse_part, precision=HIGHEST))
    root_part, inverse_part = lax.fori_loop(0, ITERS, newton, (system / frobenius, identity))
    inverse_root = inverse_part / jnp.sqrt(frobenius)
    mean_weights = jnp.dot(inverse_root, jnp.dot(inverse_root, vector, precision=HIGHEST), precision=HIGHEST)
    transform = (jnp.sqrt(SAMPLE_TOTAL - 1.0) * inverse_root + mean_weights[:, None]).astype(jnp.bfloat16)
    cells_full = patch_cells.astype(jnp.float32)
    state_mean = lax.optimization_barrier(jnp.mean(cells_full, axis=0))
    deviation = (cells_full - state_mean[None, :]).astype(jnp.bfloat16)
    moved = jnp.dot(transform.astype(jnp.float32).T, deviation.astype(jnp.float32), precision=HIGHEST)
    return (state_mean[None, :] + moved).astype(jnp.bfloat16)

def reference(prior_samples, diffusivity_field, measured_site_position, measured_quantities, measurement_weightings):
    advanced_sample = lax.map(lambda sample_label: advance_prior(sample_label, diffusivity_field), prior_samples)
    patches = advanced_sample.reshape(SAMPLE_TOTAL, BLOCKS_A, A_DEV, BLOCKS_B, B_DEV).transpose(1, 3, 0, 2, 4)
    patches = patches.reshape(BLOCKS_A, BLOCKS_B, SAMPLE_TOTAL, A_DEV * B_DEV)
    own_grams, own_vectors = lax.map(lambda group: jax.vmap(observe)(*group), (patches, measured_site_position, measured_quantities, measurement_weightings))
    padded_grams = jnp.pad(own_grams, ((1, 1), (1, 1), (0, 0), (0, 0)))
    padded_vectors = jnp.pad(own_vectors, ((1, 1), (1, 1), (0, 0)))
    gram = jnp.zeros_like(own_grams)
    vector = jnp.zeros_like(own_vectors)
    for first in range(3):
        for second in range(3):
            gram = gram + LOCALITY[first][second] * padded_grams[first:first + BLOCKS_A, second:second + BLOCKS_B]
            vector = vector + LOCALITY[first][second] * padded_vectors[first:first + BLOCKS_A, second:second + BLOCKS_B]
    updated = lax.map(lambda group: jax.vmap(analyse)(*group), (patches, gram, vector))
    updated = updated.reshape(BLOCKS_A, BLOCKS_B, SAMPLE_TOTAL, A_DEV, B_DEV).transpose(2, 0, 3, 1, 4).reshape(SAMPLE_TOTAL, MESH_HEIGHT, MESH_WIDTH)
    return lax.map(lambda sample_label: finish(sample_label, diffusivity_field), updated)
```

```python
import functools
import math

import jax
import jax.numpy as jnp
from jax import lax
from jax.experimental import pallas as pl
from jax.experimental.pallas import tpu as pltpu
from jax.sharding import PartitionSpec as P

ITERS = 10
PAD = 128
F32 = jnp.float32
BF16 = jnp.bfloat16
MESH = pl.DeviceIdType.MESH
VMEM = pl.BlockSpec(memory_space=pltpu.VMEM)
HBM = pl.BlockSpec(memory_space=pltpu.HBM)
CHUNKS = 4


def swap_matrix(outer, inner):
    size = outer * inner
    row = lax.broadcasted_iota(jnp.int32, (size, size), 0)
    column = lax.broadcasted_iota(jnp.int32, (size, size), 1)
    source = (row % inner) * outer + row // inner
    return (source == column).astype(F32).astype(BF16)


def merged(block):
    a, m, c = block.shape
    if m % 16 == 0:
        return block.reshape(a * m, c)
    return block.astype(F32).reshape(a * m, c).astype(BF16)


def halves(value):
    high = value.astype(BF16)
    return high, (value - high.astype(F32)).astype(BF16)


def dot1(a, b):
    return jnp.dot(a, b, preferred_element_type=F32)


def dot3(a, b):
    ah, al = a
    bh, bl = b
    return dot1(ah, bh) + (dot1(ah, bl) + dot1(al, bh))


def step(src, row, diffusion, at, cols):
    lo = PAD + at
    mid = src[row, :, lo : lo + cols]
    around = (
        src[row - 1, :, lo : lo + cols]
        + src[row + 1, :, lo : lo + cols]
        + src[row, :, lo - 1 : lo - 1 + cols]
        + src[row, :, lo + 1 : lo + 1 + cols]
    )
    return mid + diffusion * (around - 4.0 * mid)


def clear_pads(buf, width):
    rows, m, _ = buf.shape
    buf[:, :, :PAD] = jnp.zeros((rows, m, PAD), F32)
    buf[:, :, PAD + width :] = jnp.zeros((rows, m, PAD), F32)


class Peers:
    def __init__(self, n, spaces):
        self.n = n
        self.me = lax.axis_index("mem")
        self.space = lax.axis_index("space")
        self.has_low = self.space > 0
        self.has_high = self.space < spaces - 1
        self.order = []
        for k in range(1, n):
            peer, bit = self.me, 1
            while bit < n:
                if k & bit:
                    peer = peer + bit * (1 - 2 * ((self.me // bit) % 2))
                bit *= 2
            self.order.append(peer)

    def sides(self):
        return ((self.has_low, self.space - 1), (self.has_high, self.space + 1))

    def greet(self):
        barrier = pltpu.get_barrier_semaphore()
        for peer in self.order:
            pl.semaphore_signal(barrier, inc=1, device_id={"mem": peer}, device_id_type=MESH)
        for has, other in self.sides():

            @pl.when(has)
            def _():
                pl.semaphore_signal(barrier, inc=1, device_id={"space": other}, device_id_type=MESH)

    def meet(self):
        barrier = pltpu.get_barrier_semaphore()
        beside = self.has_low.astype(jnp.int32) + self.has_high.astype(jnp.int32)
        pl.semaphore_wait(barrier, self.n - 1 + beside)


class Blocks:
    def __init__(self, peers, src, dst, groups, send, recv):
        self.peers, self.src, self.dst = peers, src, dst
        self.groups, self.sems = groups, (send, recv)

    def copy(self, g, i, slot):
        first, last = self.groups[g]
        peer = self.peers.order[i]
        send, recv = self.sems
        return pltpu.make_async_remote_copy(
            src_ref=self.src.at[peer, first:last],
            dst_ref=self.dst.at[slot, first:last],
            send_sem=send.at[g, i],
            recv_sem=recv.at[g, i],
            device_id={"mem": peer},
            device_id_type=MESH,
        )

    def start(self, g):
        for i in range(len(self.peers.order)):
            self.copy(g, i, self.peers.me).start()
        first, last = self.groups[g]
        me = self.peers.me
        self.dst[me, first:last] = self.src[me, first:last]

    def arrive(self, g):
        for i in range(len(self.peers.order)):
            self.copy(g, i, self.peers.order[i]).wait_recv()

    def finish(self):
        for g in range(len(self.groups)):
            for i in range(len(self.peers.order)):
                self.copy(g, i, self.peers.me).wait_send()


class Rows:
    def __init__(self, peers, src, dst, send, recv):
        self.peers, self.src, self.dst = peers, src, dst
        self.send, self.recv = send, recv

    def copy(self, i, slot):
        peer = self.peers.order[i]
        return pltpu.make_async_remote_copy(
            src_ref=self.src(peer),
            dst_ref=self.dst.at[slot],
            send_sem=self.send.at[i],
            recv_sem=self.recv.at[i],
            device_id={"mem": peer},
            device_id_type=MESH,
        )

    def start(self):
        for i in range(len(self.peers.order)):
            self.copy(i, self.peers.me).start()

    def arrive(self):
        for i in range(len(self.peers.order)):
            self.copy(i, self.peers.order[i]).wait_recv()

    def finish(self):
        for i in range(len(self.peers.order)):
            self.copy(i, self.peers.me).wait_send()


def beside(src, dst, sems, slot, other):
    send, recv = sems
    return pltpu.make_async_remote_copy(
        src_ref=src,
        dst_ref=dst,
        send_sem=send.at[slot],
        recv_sem=recv.at[slot],
        device_id={"space": other},
        device_id_type=MESH,
    )


def cut(first, last, parts):
    size = -(-(last - first) // parts)
    return [(a, min(a + size, last)) for a in range(first, last, size)]


def transform_of(gram, vector, members):
    identity = (
        lax.broadcasted_iota(jnp.int32, (members, members), 0)
        == lax.broadcasted_iota(jnp.int32, (members, members), 1)
    ).astype(F32)
    system = gram + (members - 1.0) * identity
    frob = jnp.sqrt(jnp.sum(jnp.sum(system * system, axis=1, keepdims=True), axis=0, keepdims=True))
    root_part = system / frob
    factor = 1.5 * identity - 0.5 * root_part
    root_part = dot3(halves(root_part), halves(factor))
    inverse_part = factor
    for index in range(1, ITERS):
        r, z = halves(root_part), halves(inverse_part)
        f = halves(1.5 * identity - 0.5 * dot3(z, r))
        if index < ITERS - 1:
            root_part = dot3(r, f)
        inverse_part = dot3(f, z)
    inverse_root = inverse_part / jnp.sqrt(frob)
    z = halves(inverse_root)
    weights = dot3(halves(dot3(halves(vector), z)), z)[0:1, :]
    return (math.sqrt(members - 1.0) * inverse_root + weights).astype(BF16)


LEAD, BEFORE = 2, 1


def row_groups(rows):
    return [(4,6),(6,10),(0,4),(10,13),(13,16)]


def return_groups(rows):
    middle = cut(4, rows, 3)
    return [(0, 4), *middle[:-1], *cut(*middle[-1], 2)]


def swap_kernel(moved_ref, out_ref, swap):
    rows, m, _ = moved_ref.shape

    @pl.when(pl.program_id(0) == 0)
    def _():
        swap[...] = swap_matrix(m, rows)

    out_ref[...] = dot1(swap[...], merged(moved_ref[...])).astype(BF16)


def cycle_kernel(
    spaces, x_hbm, d_hbm, site_hbm, value_hbm, weight_hbm, moved_hbm,
    x_ref, d_ref, value_ref, weight_ref, moved, load, store,
    xs, v1, fresh, patch, updated, back, edge_out, edge_in, d_out, d_in, last_in,
    sites, seen_out, seen, gram_out, gram_in, turned,
    send, recv, return_send, return_recv, side_send, side_recv,
    site_send, site_recv, seen_send, seen_recv, gram_send, gram_recv,
):
    patches, rows, m, cols = patch.shape
    width = patches * cols
    members = patches * m
    obs = value_ref.shape[1]
    peers = Peers(patches, spaces)
    me = peers.me
    part = width // CHUNKS
    loads = [
        pltpu.make_async_copy(
            x_hbm.at[:, c * part : (c + 1) * part], x_ref.at[:, c * part : (c + 1) * part], load.at[c]
        )
        for c in range(CHUNKS)
    ]
    loads += [
        pltpu.make_async_copy(src, dst, load.at[CHUNKS + i])
        for i, (src, dst) in enumerate(
            (
                (d_hbm, d_ref),
                (site_hbm, sites.at[me]),
                (value_hbm, value_ref),
                (weight_hbm, weight_ref),
            )
        )
    ]
    for copy in loads:
        copy.start()
    peers.greet()
    groups = row_groups(rows)
    middle = [group for group in groups if group[0] > 0]
    blocks = Blocks(peers, fresh, patch, groups, send, recv)
    returned = return_groups(rows)
    returns = Blocks(peers, updated, back, returned, return_send, return_recv)
    site_blocks = Rows(peers, lambda peer: sites.at[me], sites, site_send, site_recv)
    seen_blocks = Rows(peers, lambda peer: seen_out.at[peer], seen, seen_send, seen_recv)
    side = (side_send, side_recv)
    sides = list(enumerate(peers.sides()))

    swap = swap_matrix(rows, m)
    clear_pads(xs, width)
    clear_pads(v1, width)
    for at in range(0, width, 2 * cols):
        if at % part == 0:
            loads[at // part].wait()
        turn = dot1(swap, x_ref[:, at : at + 2 * cols]).reshape(rows, m, 2 * cols)
        xs[2 : rows + 2, :, PAD + at : PAD + at + 2 * cols] = turn
        edge_out[0, :, :, at : at + 2 * cols] = turn[:2].astype(BF16)
        edge_out[1, :, :, at : at + 2 * cols] = turn[rows - 2 :].astype(BF16)
    for copy in loads[CHUNKS:]:
        copy.wait()
    d_out[0] = d_ref[0:1, :]
    d_out[1] = d_ref[rows - 1 : rows, :]

    peers.meet()

    def halo(k, other):
        return (
            beside(edge_out.at[k], edge_in.at[1 - k], side, k, other),
            beside(d_out.at[k], d_in.at[1 - k], side, 2 + k, other),
        )

    def halo_in(k, other):
        return (
            beside(edge_out.at[k], edge_in.at[k], side, 1 - k, other),
            beside(d_out.at[k], d_in.at[k], side, 3 - k, other),
        )

    for k, (has, other) in sides:

        @pl.when(has)
        def _():
            for copy in halo(k, other):
                copy.start()

    site_blocks.start()

    def first_step(r, d_row):
        for q in range(patches):
            at = q * cols
            v1[r, :, PAD + at : PAD + at + cols] = step(xs, r, d_row(at), at, cols)

    def second_step(r, place):
        for q in range(patches):
            at = q * cols
            d_row = d_ref[pl.ds(r - 2, 1), at : at + cols]
            fresh[q, place] = step(v1, r, d_row, at, cols).astype(BF16)

    done = 3
    for g, (first, last) in enumerate(middle):

        @pl.loop(done, last + 1)
        def _(r):
            first_step(r, lambda at: d_ref[pl.ds(r - 2, 1), at : at + cols])

        done = last + 1

        @pl.loop(first, last)
        def _(r):
            second_step(r, r)

        if g < LEAD:
            blocks.start(g)

    for k, (has, other) in sides:
        row = 0 if k == 0 else rows + 2

        @pl.when(has)
        def _():
            for copy in halo_in(k, other):
                copy.wait_recv()
            xs[row : row + 2, :, PAD : PAD + width] = edge_in[k].astype(F32)

        @pl.when(jnp.logical_not(has))
        def _():
            xs[row : row + 2, :, PAD : PAD + width] = jnp.zeros((2, m, width), F32)
            d_in[k] = jnp.zeros((1, width), F32)

        outer, inner = (1, 2) if k == 0 else (rows + 2, rows + 1)
        first_step(outer, lambda at: d_in[k, :, at : at + cols])
        first_step(inner, lambda at: d_ref[inner - 2 : inner - 1, at : at + cols])

        for r in (2, 3) if k == 0 else (rows, rows + 1):
            second_step(r, r % rows)

    site_blocks.arrive()

    @pl.loop(0, patches)
    def _(q):
        lanes = 128
        at = [
            jnp.broadcast_to(sites[q, :, o * lanes : (o + 1) * lanes], (m, lanes))
            for o in range(obs // lanes)
        ]
        lane = [v % lanes for v in at]
        tile = [v // lanes for v in at]
        picked = [jnp.zeros((m, lanes), F32) for _ in at]
        for r in range(rows):
            for h in range(cols // lanes):
                cells = fresh[q, (r + 2) % rows, :, h * lanes : (h + 1) * lanes].astype(F32)
                number = r * (cols // lanes) + h
                for o in range(len(at)):
                    got = jnp.take_along_axis(cells, lane[o], axis=1, mode="promise_in_bounds")
                    picked[o] = jnp.where(tile[o] == number, got, picked[o])
        for o in range(len(at)):
            seen_out[q, :, o * lanes : (o + 1) * lanes] = picked[o].astype(BF16)

    seen_blocks.start()
    seen[me] = seen_out[me]
    for g in range(LEAD, LEAD + BEFORE):
        blocks.start(g)
    seen_blocks.arrive()

    observed = merged(seen[...]).astype(F32)
    obs_mean = jnp.sum(observed, axis=0, keepdims=True) * (1.0 / members)
    root = jnp.sqrt(weight_ref[...])
    spread = ((observed - obs_mean) * root).astype(BF16)
    innovation = ((value_ref[...] - obs_mean) * root).astype(BF16)
    contract = (((1,), (1,)), ((), ()))
    gram_out[0, 0:members, :] = lax.dot_general(
        spread, spread, contract, preferred_element_type=F32
    )
    wide = jnp.broadcast_to(innovation.astype(F32), (8, obs)).astype(BF16)
    gram_out[0, members : members + 8, :] = lax.dot_general(
        wide, spread, contract, preferred_element_type=F32
    )

    def to_beside(stage, k, axis, other):
        return pltpu.make_async_remote_copy(
            src_ref=gram_out.at[stage],
            dst_ref=gram_in.at[stage, 1 - k],
            send_sem=gram_send.at[stage, k],
            recv_sem=gram_recv.at[stage, 1 - k],
            device_id={axis: other},
            device_id_type=MESH,
        )

    def from_beside(stage, k, axis, other):
        return pltpu.make_async_remote_copy(
            src_ref=gram_out.at[stage],
            dst_ref=gram_in.at[stage, k],
            send_sem=gram_send.at[stage, k],
            recv_sem=gram_recv.at[stage, k],
            device_id={axis: other},
            device_id_type=MESH,
        )

    def gram_send_all(stage, axis, pairs):
        for k, (has, other) in enumerate(pairs):

            @pl.when(has)
            def _():
                to_beside(stage, k, axis, other).start()

            @pl.when(jnp.logical_not(has))
            def _():
                gram_in[stage, k] = jnp.zeros((members + 8, members), F32)

    def gram_sum(stage, axis, pairs):
        for k, (has, other) in enumerate(pairs):

            @pl.when(has)
            def _():
                from_beside(stage, k, axis, other).wait_recv()

        return gram_out[stage] + 0.5 * (gram_in[stage, 0] + gram_in[stage, 1])

    along = ((me > 0, me - 1), (me < patches - 1, me + 1))
    gram_send_all(0, "mem", along)
    for g in range(LEAD + BEFORE, len(groups)):
        blocks.start(g)
    gram_out[1] = gram_sum(0, "mem", along)
    gram_send_all(1, "space", peers.sides())
    gram_out[2] = gram_sum(1, "space", peers.sides())
    turned[...] = transform_of(gram_out[2, 0:members], gram_out[2, members:], members)

    arrived = set()
    for g, (first, last) in enumerate(returned):
        index = max(i for i, (low, high) in enumerate(groups) if low < last and high > first)
        for earlier in range(index + 1):
            if earlier not in arrived:
                blocks.arrive(earlier)
                arrived.add(earlier)

        @pl.loop(first, last)
        def _(r):
            cells = merged(patch[:, r]).astype(F32)
            mean = jnp.sum(cells, axis=0, keepdims=True) * (1.0 / members)
            result = mean + dot1(turned[...], (cells - mean).astype(BF16))
            updated[:, r] = result.reshape(patches, m, cols).astype(BF16)

        returns.start(g)

    def last_halo(k, other):
        row = 2 if k == 0 else 1
        return beside(back.at[:, row], last_in.at[1 - k], side, 4 + k, other)

    def last_halo_in(k, other):
        return beside(back.at[:, 0], last_in.at[k], side, 5 - k, other)

    def take(r, place):
        for q in range(patches):
            xs[r + 1, :, PAD + q * cols : PAD + (q + 1) * cols] = back[q, place].astype(F32)

    def stored(r):
        return pltpu.make_async_copy(moved.at[r], moved_hbm.at[r], store.at[r])

    def last_step(r, d_row):
        for q in range(patches):
            at = q * cols
            moved[r, :, at : at + cols] = step(xs, r + 1, d_row(at), at, cols).astype(BF16)
        stored(r).start()

    returns.arrive(0)
    for k, (has, other) in sides:

        @pl.when(has)
        def _():
            last_halo(k, other).start()

        for r in (0, 1) if k == 0 else (rows - 2, rows - 1):
            take(r, (r + 2) % rows)

    done = 1
    for g in range(1, len(returned)):
        first, last = returned[g]
        returns.arrive(g)

        @pl.loop(first, last)
        def _(r):
            take(r - 2, r)

        upto = rows - 1 if g == len(returned) - 1 else last - 3

        @pl.loop(done, upto)
        def _(r):
            last_step(r, lambda at: d_ref[pl.ds(r, 1), at : at + cols])

        done = upto
        if g == 1:
            for k, (has, other) in sides:
                row = 0 if k == 0 else rows + 1

                @pl.when(has)
                def _():
                    last_halo_in(k, other).wait_recv()
                    for q in range(patches):
                        xs[row, :, PAD + q * cols : PAD + (q + 1) * cols] = last_in[k, q].astype(F32)

                @pl.when(jnp.logical_not(has))
                def _():
                    xs[row, :, PAD : PAD + width] = jnp.zeros((m, width), F32)

                r = 0 if k == 0 else rows - 1
                last_step(r, lambda at: d_ref[r : r + 1, at : at + cols])

    @pl.loop(0, rows)
    def _(r):
        stored(r).wait()

    for sent in (blocks, returns, site_blocks, seen_blocks):
        sent.finish()
    for k, (has, other) in sides:

        @pl.when(has)
        def _():
            for copy in (*halo(k, other), last_halo(k, other)):
                copy.wait_send()

    for stage, axis, pairs in ((0, "mem", along), (1, "space", peers.sides())):
        for k, (has, other) in enumerate(pairs):

            @pl.when(has)
            def _():
                to_beside(stage, k, axis, other).wait_send()


def body(prior, diffusivity, site, quantities, weightings):
    m, rows, width = prior.shape
    patches = lax.axis_size("mem")
    spaces = lax.axis_size("space")
    cols = width // patches
    members = m * patches
    obs = site.shape[-1]
    padded = width + 2 * PAD
    dma = pltpu.SemaphoreType.DMA
    many = len(row_groups(rows))
    others = patches - 1
    args = (
        prior.reshape(m * rows, width),
        diffusivity,
        site[0],
        quantities[0],
        weightings[0],
    )
    bulk = pltpu.VMEM((patches, rows, m, cols), BF16)
    moved = pl.pallas_call(
        functools.partial(cycle_kernel, spaces),
        out_shape=jax.ShapeDtypeStruct((rows, m, width), BF16),
        in_specs=[HBM] * len(args),
        out_specs=HBM,
        scratch_shapes=[
            pltpu.VMEM((m * rows, width), BF16),
            pltpu.VMEM((rows, width), F32),
            pltpu.VMEM((1, obs), F32),
            pltpu.VMEM((1, obs), F32),
            pltpu.VMEM((rows, m, width), BF16),
            dma((CHUNKS + 4,)),
            dma((rows,)),
            pltpu.VMEM((rows + 4, m, padded), F32),
            pltpu.VMEM((rows + 4, m, padded), F32),
            bulk,
            bulk,
            bulk,
            bulk,
            pltpu.VMEM((2, 2, m, width), BF16),
            pltpu.VMEM((2, 2, m, width), BF16),
            pltpu.VMEM((2, 1, width), F32),
            pltpu.VMEM((2, 1, width), F32),
            pltpu.VMEM((2, patches, m, cols), BF16),
            pltpu.VMEM((patches, 1, obs), jnp.int32),
            pltpu.VMEM((patches, m, obs), BF16),
            pltpu.VMEM((patches, m, obs), BF16),
            pltpu.VMEM((3, members + 8, members), F32),
            pltpu.VMEM((2, 2, members + 8, members), F32),
            pltpu.VMEM((members, members), BF16),
            *[dma((many, others))] * 2,
            *[dma((len(return_groups(rows)), others))] * 2,
            dma((6,)),
            dma((6,)),
            *[dma((others,))] * 4,
            dma((2, 2)),
            dma((2, 2)),
        ],
        compiler_params=pltpu.CompilerParams(
            vmem_limit_bytes=58 * 2**20, collective_id=0, has_side_effects=True
        ),
        name="cycle",
    )(*args)
    size, lanes = m * rows, width // 4
    out = pl.pallas_call(
        swap_kernel,
        out_shape=jax.ShapeDtypeStruct((size, width), BF16),
        grid=(4,),
        in_specs=[
            pl.BlockSpec((rows, m, lanes), lambda c: (0, 0, c)),
        ],
        out_specs=pl.BlockSpec((size, lanes), lambda c: (0, c)),
        scratch_shapes=[pltpu.VMEM((size, size), BF16)],
        compiler_params=pltpu.CompilerParams(vmem_limit_bytes=58 * 2**20),
        name="swap",
    )(moved)
    return out.reshape(m, rows, width)


def solution(mesh):
    return jax.shard_map(
        body,
        mesh=mesh,
        in_specs=(
            P("mem", "space", None),
            P("space", None),
            P("space", "mem", None),
            P("space", "mem", None),
            P("space", "mem", None),
        ),
        out_specs=P("mem", "space", None),
        check_vma=False,
    )
```

```python
import functools
import math

import jax
import jax.numpy as jnp
from jax import lax
from jax.experimental import pallas as pl
from jax.experimental.pallas import tpu as pltpu
from jax.sharding import PartitionSpec as P

ITERS = 10
PAD = 128
F32 = jnp.float32
BF16 = jnp.bfloat16
MESH = pl.DeviceIdType.MESH
VMEM = pl.BlockSpec(memory_space=pltpu.VMEM)
HBM = pl.BlockSpec(memory_space=pltpu.HBM)
CHUNKS = 4


def swap_matrix(outer, inner):
    size = outer * inner
    row = lax.broadcasted_iota(jnp.int32, (size, size), 0)
    column = lax.broadcasted_iota(jnp.int32, (size, size), 1)
    source = (row % inner) * outer + row // inner
    return (source == column).astype(F32).astype(BF16)


def merged(block):
    a, m, c = block.shape
    if m % 16 == 0:
        return block.reshape(a * m, c)
    return block.astype(F32).reshape(a * m, c).astype(BF16)


def halves(value):
    high = value.astype(BF16)
    return high, (value - high.astype(F32)).astype(BF16)


def dot1(a, b):
    return jnp.dot(a, b, preferred_element_type=F32)


def dot3(a, b):
    ah, al = a
    bh, bl = b
    return dot1(ah, bh) + (dot1(ah, bl) + dot1(al, bh))


def step(src, row, diffusion, at, cols):
    lo = PAD + at
    mid = src[row, :, lo : lo + cols]
    around = (
        src[row - 1, :, lo : lo + cols]
        + src[row + 1, :, lo : lo + cols]
        + src[row, :, lo - 1 : lo - 1 + cols]
        + src[row, :, lo + 1 : lo + 1 + cols]
    )
    return mid + diffusion * (around - 4.0 * mid)


def clear_pads(buf, width):
    rows, m, _ = buf.shape
    buf[:, :, :PAD] = jnp.zeros((rows, m, PAD), F32)
    buf[:, :, PAD + width :] = jnp.zeros((rows, m, PAD), F32)


class Peers:
    def __init__(self, n, spaces):
        self.n = n
        self.me = lax.axis_index("mem")
        self.space = lax.axis_index("space")
        self.has_low = self.space > 0
        self.has_high = self.space < spaces - 1
        self.order = []
        for k in range(1, n):
            peer, bit = self.me, 1
            while bit < n:
                if k & bit:
                    peer = peer + bit * (1 - 2 * ((self.me // bit) % 2))
                bit *= 2
            self.order.append(peer)

    def sides(self):
        return ((self.has_low, self.space - 1), (self.has_high, self.space + 1))

    def greet(self):
        barrier = pltpu.get_barrier_semaphore()
        for peer in self.order:
            pl.semaphore_signal(barrier, inc=1, device_id={"mem": peer}, device_id_type=MESH)
        for has, other in self.sides():

            @pl.when(has)
            def _():
                pl.semaphore_signal(barrier, inc=1, device_id={"space": other}, device_id_type=MESH)

    def meet(self):
        barrier = pltpu.get_barrier_semaphore()
        beside = self.has_low.astype(jnp.int32) + self.has_high.astype(jnp.int32)
        pl.semaphore_wait(barrier, self.n - 1 + beside)


class Blocks:
    def __init__(self, peers, src, dst, groups, send, recv):
        self.peers, self.src, self.dst = peers, src, dst
        self.groups, self.sems = groups, (send, recv)

    def copy(self, g, i, slot):
        first, last = self.groups[g]
        peer = self.peers.order[i]
        send, recv = self.sems
        return pltpu.make_async_remote_copy(
            src_ref=self.src.at[peer, first:last],
            dst_ref=self.dst.at[slot, first:last],
            send_sem=send.at[g, i],
            recv_sem=recv.at[g, i],
            device_id={"mem": peer},
            device_id_type=MESH,
        )

    def start(self, g):
        for i in range(len(self.peers.order)):
            self.copy(g, i, self.peers.me).start()
        first, last = self.groups[g]
        me = self.peers.me
        self.dst[me, first:last] = self.src[me, first:last]

    def arrive(self, g):
        for i in range(len(self.peers.order)):
            self.copy(g, i, self.peers.order[i]).wait_recv()

    def finish(self):
        for g in range(len(self.groups)):
            for i in range(len(self.peers.order)):
                self.copy(g, i, self.peers.me).wait_send()


class Rows:
    def __init__(self, peers, src, dst, send, recv):
        self.peers, self.src, self.dst = peers, src, dst
        self.send, self.recv = send, recv

    def copy(self, i, slot):
        peer = self.peers.order[i]
        return pltpu.make_async_remote_copy(
            src_ref=self.src(peer),
            dst_ref=self.dst.at[slot],
            send_sem=self.send.at[i],
            recv_sem=self.recv.at[i],
            device_id={"mem": peer},
            device_id_type=MESH,
        )

    def start(self):
        for i in range(len(self.peers.order)):
            self.copy(i, self.peers.me).start()

    def arrive(self):
        for i in range(len(self.peers.order)):
            self.copy(i, self.peers.order[i]).wait_recv()

    def finish(self):
        for i in range(len(self.peers.order)):
            self.copy(i, self.peers.me).wait_send()


def beside(src, dst, sems, slot, other):
    send, recv = sems
    return pltpu.make_async_remote_copy(
        src_ref=src,
        dst_ref=dst,
        send_sem=send.at[slot],
        recv_sem=recv.at[slot],
        device_id={"space": other},
        device_id_type=MESH,
    )


def cut(first, last, parts):
    size = -(-(last - first) // parts)
    return [(a, min(a + size, last)) for a in range(first, last, size)]


def packed(gram):
    half = gram.shape[0] // 2
    row = lax.broadcasted_iota(jnp.int32, (half, half), 0)
    column = lax.broadcasted_iota(jnp.int32, (half, half), 1)
    last = gram[half:, half:]
    both = jnp.where(row <= column, gram[:half, :half], last)
    diagonal = jnp.sum(jnp.where(row == column, last, 0.0), axis=0, keepdims=True)
    return both, gram[:half, half:], diagonal


def unpacked(both, cross, diagonal):
    half = both.shape[0]
    row = lax.broadcasted_iota(jnp.int32, (half, half), 0)
    column = lax.broadcasted_iota(jnp.int32, (half, half), 1)
    turned = both.T
    first = jnp.where(row <= column, both, turned)
    last = jnp.where(row > column, both, jnp.where(row == column, diagonal, turned))
    top = jnp.concatenate([first, cross], axis=1)
    return jnp.concatenate([top, jnp.concatenate([cross.T, last], axis=1)], axis=0)


def transform_of(gram, vector, members):
    identity = (
        lax.broadcasted_iota(jnp.int32, (members, members), 0)
        == lax.broadcasted_iota(jnp.int32, (members, members), 1)
    ).astype(F32)
    system = gram + (members - 1.0) * identity
    frob = jnp.sqrt(jnp.sum(jnp.sum(system * system, axis=1, keepdims=True), axis=0, keepdims=True))
    root_part = system / frob
    factor = 1.5 * identity - 0.5 * root_part
    root_part = dot3(halves(root_part), halves(factor))
    inverse_part = factor
    for index in range(1, ITERS):
        r, z = halves(root_part), halves(inverse_part)
        f = halves(1.5 * identity - 0.5 * dot3(z, r))
        if index < ITERS - 1:
            root_part = dot3(r, f)
        inverse_part = dot3(f, z)
    inverse_root = inverse_part / jnp.sqrt(frob)
    z = halves(inverse_root)
    weights = dot3(halves(dot3(halves(vector), z)), z)[0:1, :]
    return (math.sqrt(members - 1.0) * inverse_root + weights).astype(BF16)


LEAD, BEFORE = 2, 1


def row_groups(rows):
    middle = rows - 4
    low, high = 4 + middle // 6, 4 + middle // 2
    return [(4, low), (low, high), (0, 4), (high, rows)]


def return_groups(rows):
    return [(0, 4), *cut(4, rows, 3)]


def swap_kernel(moved, out_hbm, out, store):
    rows, m, width = moved.shape
    part = width // CHUNKS
    spans = [pl.ds(c * part, part) for c in range(CHUNKS)]
    stores = [
        pltpu.make_async_copy(out.at[:, span], out_hbm.at[:, span], store.at[c])
        for c, span in enumerate(spans)
    ]
    swap = swap_matrix(m, rows)
    for span, leaving in zip(spans, stores):
        out[:, span] = dot1(swap, merged(moved[:, :, span])).astype(BF16)
        leaving.start()
    for copy in stores:
        copy.wait()


def cycle_kernel(
    spaces, x_hbm, d_hbm, site_hbm, value_hbm, weight_hbm, moved,
    x_ref, d_ref, value_ref, weight_ref, load,
    xs, v1, fresh, patch, updated, back, edge_out, edge_in, d_out, d_in, last_in,
    sites, seen_out, seen, gram_out, gram_in, turned,
    send, recv, return_send, return_recv, side_send, side_recv,
    site_send, site_recv, seen_send, seen_recv, gram_send, gram_recv,
):
    patches, rows, m, cols = patch.shape
    width = patches * cols
    members = patches * m
    obs = value_ref.shape[1]
    peers = Peers(patches, spaces)
    me = peers.me
    part = width // CHUNKS
    loads = [
        pltpu.make_async_copy(
            x_hbm.at[:, c * part : (c + 1) * part], x_ref.at[:, c * part : (c + 1) * part], load.at[c]
        )
        for c in range(CHUNKS)
    ]
    loads += [
        pltpu.make_async_copy(src, dst, load.at[CHUNKS + i])
        for i, (src, dst) in enumerate(
            (
                (d_hbm, d_ref),
                (site_hbm, sites.at[me]),
                (value_hbm, value_ref),
                (weight_hbm, weight_ref),
            )
        )
    ]
    for copy in loads:
        copy.start()
    peers.greet()
    groups = row_groups(rows)
    middle = [group for group in groups if group[0] > 0]
    blocks = Blocks(peers, fresh, patch, groups, send, recv)
    returned = return_groups(rows)
    returns = Blocks(peers, updated, back, returned, return_send, return_recv)
    site_blocks = Rows(peers, lambda peer: sites.at[me], sites, site_send, site_recv)
    seen_blocks = Rows(peers, lambda peer: seen_out.at[peer], seen, seen_send, seen_recv)
    side = (side_send, side_recv)
    sides = list(enumerate(peers.sides()))

    swap = swap_matrix(rows, m)
    clear_pads(xs, width)
    clear_pads(v1, width)
    for at in range(0, width, 2 * cols):
        if at % part == 0:
            loads[at // part].wait()
        turn = dot1(swap, x_ref[:, at : at + 2 * cols]).reshape(rows, m, 2 * cols)
        xs[2 : rows + 2, :, PAD + at : PAD + at + 2 * cols] = turn
        edge_out[0, :, :, at : at + 2 * cols] = turn[:2].astype(BF16)
        edge_out[1, :, :, at : at + 2 * cols] = turn[rows - 2 :].astype(BF16)
    for copy in loads[CHUNKS:]:
        copy.wait()
    d_out[0] = d_ref[0:1, :]
    d_out[1] = d_ref[rows - 1 : rows, :]

    def halo(k, other):
        return (
            beside(edge_out.at[k], edge_in.at[1 - k], side, k, other),
            beside(d_out.at[k], d_in.at[1 - k], side, 2 + k, other),
        )

    def halo_in(k, other):
        return (
            beside(edge_out.at[k], edge_in.at[k], side, 1 - k, other),
            beside(d_out.at[k], d_in.at[k], side, 3 - k, other),
        )

    def first_step(r, d_row):
        for q in range(patches):
            at = q * cols
            v1[r, :, PAD + at : PAD + at + cols] = step(xs, r, d_row(at), at, cols)

    def second_step(r, place):
        for q in range(patches):
            at = q * cols
            d_row = d_ref[pl.ds(r - 2, 1), at : at + cols]
            fresh[q, place] = step(v1, r, d_row, at, cols).astype(BF16)

    done = 3
    for g, (first, last) in enumerate(middle):

        @pl.loop(done, last + 1)
        def _(r):
            first_step(r, lambda at: d_ref[pl.ds(r - 2, 1), at : at + cols])

        done = last + 1

        @pl.loop(first, last)
        def _(r):
            second_step(r, r)

        if g == 0:
            peers.meet()
            for k, (has, other) in sides:

                @pl.when(has)
                def _():
                    for copy in halo(k, other):
                        copy.start()

        if g < LEAD:
            blocks.start(g)
        if g == 0:
            site_blocks.start()

    for k, (has, other) in sides:
        row = 0 if k == 0 else rows + 2

        @pl.when(has)
        def _():
            for copy in halo_in(k, other):
                copy.wait_recv()
            xs[row : row + 2, :, PAD : PAD + width] = edge_in[k].astype(F32)

        @pl.when(jnp.logical_not(has))
        def _():
            xs[row : row + 2, :, PAD : PAD + width] = jnp.zeros((2, m, width), F32)
            d_in[k] = jnp.zeros((1, width), F32)

        outer, inner = (1, 2) if k == 0 else (rows + 2, rows + 1)
        first_step(outer, lambda at: d_in[k, :, at : at + cols])
        first_step(inner, lambda at: d_ref[inner - 2 : inner - 1, at : at + cols])

        for r in (2, 3) if k == 0 else (rows, rows + 1):
            second_step(r, r % rows)

    site_blocks.arrive()

    @pl.loop(0, patches)
    def _(q):
        lanes = 128
        at = [
            jnp.broadcast_to(sites[q, :, o * lanes : (o + 1) * lanes], (m, lanes))
            for o in range(obs // lanes)
        ]
        lane = [v % lanes for v in at]
        tile = [v // lanes for v in at]
        picked = [jnp.zeros((m, lanes), F32) for _ in at]
        for r in range(rows):
            for h in range(cols // lanes):
                cells = fresh[q, (r + 2) % rows, :, h * lanes : (h + 1) * lanes].astype(F32)
                number = r * (cols // lanes) + h
                for o in range(len(at)):
                    got = jnp.take_along_axis(cells, lane[o], axis=1, mode="promise_in_bounds")
                    picked[o] = jnp.where(tile[o] == number, got, picked[o])
        for o in range(len(at)):
            seen_out[q, :, o * lanes : (o + 1) * lanes] = picked[o].astype(BF16)

    seen_blocks.start()
    seen[me] = seen_out[me]
    for g in range(LEAD, LEAD + BEFORE):
        blocks.start(g)
    seen_blocks.arrive()

    observed = merged(seen[...]).astype(F32)
    obs_mean = jnp.sum(observed, axis=0, keepdims=True) * (1.0 / members)
    root = jnp.sqrt(weight_ref[...])
    spread = ((observed - obs_mean) * root).astype(BF16)
    innovation = ((value_ref[...] - obs_mean) * root).astype(BF16)
    contract = (((1,), (1,)), ((), ()))
    half = members // 2
    both, cross, diagonal = packed(
        lax.dot_general(spread, spread, contract, preferred_element_type=F32)
    )
    gram_out[0, 0:half, 0:half] = both
    gram_out[0, 0:half, half:] = cross
    wide = jnp.broadcast_to(innovation.astype(F32), (8, obs)).astype(BF16)
    gram_out[0, half : half + 8, :] = lax.dot_general(
        wide, spread, contract, preferred_element_type=F32
    )
    gram_out[0, half + 8 :, 0:half] = jnp.broadcast_to(diagonal, (8, half))
    gram_out[0, half + 8 :, half:] = jnp.zeros((8, half), F32)

    def to_beside(stage, k, axis, other):
        return pltpu.make_async_remote_copy(
            src_ref=gram_out.at[stage],
            dst_ref=gram_in.at[stage, 1 - k],
            send_sem=gram_send.at[stage, k],
            recv_sem=gram_recv.at[stage, 1 - k],
            device_id={axis: other},
            device_id_type=MESH,
        )

    def from_beside(stage, k, axis, other):
        return pltpu.make_async_remote_copy(
            src_ref=gram_out.at[stage],
            dst_ref=gram_in.at[stage, k],
            send_sem=gram_send.at[stage, k],
            recv_sem=gram_recv.at[stage, k],
            device_id={axis: other},
            device_id_type=MESH,
        )

    def gram_send_all(stage, axis, pairs):
        for k, (has, other) in enumerate(pairs):

            @pl.when(has)
            def _():
                to_beside(stage, k, axis, other).start()

            @pl.when(jnp.logical_not(has))
            def _():
                gram_in[stage, k] = jnp.zeros((half + 16, members), F32)

    def gram_sum(stage, axis, pairs):
        for k, (has, other) in enumerate(pairs):

            @pl.when(has)
            def _():
                from_beside(stage, k, axis, other).wait_recv()

        return gram_out[stage] + 0.5 * (gram_in[stage, 0] + gram_in[stage, 1])

    along = ((me > 0, me - 1), (me < patches - 1, me + 1))
    gram_send_all(0, "mem", along)
    for g in range(LEAD + BEFORE, len(groups)):
        blocks.start(g)
    gram_out[1] = gram_sum(0, "mem", along)
    gram_send_all(1, "space", peers.sides())
    gram_out[2] = gram_sum(1, "space", peers.sides())
    gram = unpacked(
        gram_out[2, 0:half, 0:half], gram_out[2, 0:half, half:], gram_out[2, half + 8 : half + 9, 0:half]
    )
    turned[...] = transform_of(gram, gram_out[2, half : half + 8], members)

    arrived = set()
    for g, (first, last) in enumerate(returned):
        index = max(i for i, (low, high) in enumerate(groups) if low < last and high > first)
        for earlier in range(index + 1):
            if earlier not in arrived:
                blocks.arrive(earlier)
                arrived.add(earlier)

        @pl.loop(first, last)
        def _(r):
            cells = merged(patch[:, r]).astype(F32)
            mean = jnp.sum(cells, axis=0, keepdims=True) * (1.0 / members)
            result = mean + dot1(turned[...], (cells - mean).astype(BF16))
            updated[:, r] = result.reshape(patches, m, cols).astype(BF16)

        returns.start(g)

    def last_halo(k, other):
        row = 2 if k == 0 else 1
        return beside(back.at[:, row], last_in.at[1 - k], side, 4 + k, other)

    def last_halo_in(k, other):
        return beside(back.at[:, 0], last_in.at[k], side, 5 - k, other)

    def take(r, place):
        for q in range(patches):
            xs[r + 1, :, PAD + q * cols : PAD + (q + 1) * cols] = back[q, place].astype(F32)

    def last_step(r, d_row):
        for q in range(patches):
            at = q * cols
            moved[r, :, at : at + cols] = step(xs, r + 1, d_row(at), at, cols).astype(BF16)

    returns.arrive(0)
    for k, (has, other) in sides:

        @pl.when(has)
        def _():
            last_halo(k, other).start()

        for r in (0, 1) if k == 0 else (rows - 2, rows - 1):
            take(r, (r + 2) % rows)

    done = 1
    for g in range(1, len(returned)):
        first, last = returned[g]
        returns.arrive(g)

        @pl.loop(first, last)
        def _(r):
            take(r - 2, r)

        upto = rows - 1 if g == len(returned) - 1 else last - 3

        @pl.loop(done, upto)
        def _(r):
            last_step(r, lambda at: d_ref[pl.ds(r, 1), at : at + cols])

        done = upto
        if g == 1:
            for k, (has, other) in sides:
                row = 0 if k == 0 else rows + 1

                @pl.when(has)
                def _():
                    last_halo_in(k, other).wait_recv()
                    for q in range(patches):
                        xs[row, :, PAD + q * cols : PAD + (q + 1) * cols] = last_in[k, q].astype(F32)

                @pl.when(jnp.logical_not(has))
                def _():
                    xs[row, :, PAD : PAD + width] = jnp.zeros((m, width), F32)

                r = 0 if k == 0 else rows - 1
                last_step(r, lambda at: d_ref[r : r + 1, at : at + cols])

    for sent in (blocks, returns, site_blocks, seen_blocks):
        sent.finish()
    for k, (has, other) in sides:

        @pl.when(has)
        def _():
            for copy in (*halo(k, other), last_halo(k, other)):
                copy.wait_send()

    for stage, axis, pairs in ((0, "mem", along), (1, "space", peers.sides())):
        for k, (has, other) in enumerate(pairs):

            @pl.when(has)
            def _():
                to_beside(stage, k, axis, other).wait_send()


def body(prior, diffusivity, site, quantities, weightings):
    m, rows, width = prior.shape
    patches = lax.axis_size("mem")
    spaces = lax.axis_size("space")
    cols = width // patches
    members = m * patches
    obs = site.shape[-1]
    padded = width + 2 * PAD
    dma = pltpu.SemaphoreType.DMA
    many = len(row_groups(rows))
    others = patches - 1
    args = (
        prior.reshape(m * rows, width),
        diffusivity,
        site[0],
        quantities[0],
        weightings[0],
    )
    bulk = pltpu.VMEM((patches, rows, m, cols), BF16)
    moved = pl.pallas_call(
        functools.partial(cycle_kernel, spaces),
        out_shape=jax.ShapeDtypeStruct((rows, m, width), BF16),
        in_specs=[HBM] * len(args),
        out_specs=VMEM,
        scratch_shapes=[
            pltpu.VMEM((m * rows, width), BF16),
            pltpu.VMEM((rows, width), F32),
            pltpu.VMEM((1, obs), F32),
            pltpu.VMEM((1, obs), F32),
            dma((CHUNKS + 4,)),
            pltpu.VMEM((rows + 4, m, padded), F32),
            pltpu.VMEM((rows + 4, m, padded), F32),
            bulk,
            bulk,
            bulk,
            bulk,
            pltpu.VMEM((2, 2, m, width), BF16),
            pltpu.VMEM((2, 2, m, width), BF16),
            pltpu.VMEM((2, 1, width), F32),
            pltpu.VMEM((2, 1, width), F32),
            pltpu.VMEM((2, patches, m, cols), BF16),
            pltpu.VMEM((patches, 1, obs), jnp.int32),
            pltpu.VMEM((patches, m, obs), BF16),
            pltpu.VMEM((patches, m, obs), BF16),
            pltpu.VMEM((3, members // 2 + 16, members), F32),
            pltpu.VMEM((2, 2, members // 2 + 16, members), F32),
            pltpu.VMEM((members, members), BF16),
            *[dma((many, others))] * 2,
            *[dma((len(return_groups(rows)), others))] * 2,
            dma((6,)),
            dma((6,)),
            *[dma((others,))] * 4,
            dma((2, 2)),
            dma((2, 2)),
        ],
        compiler_params=pltpu.CompilerParams(
            vmem_limit_bytes=44 * 2**20, collective_id=0, has_side_effects=True
        ),
        name="cycle",
    )(*(pltpu.with_memory_space_constraint(arg, pltpu.HBM) for arg in args))
    size = m * rows
    out = pl.pallas_call(
        swap_kernel,
        out_shape=jax.ShapeDtypeStruct((size, width), BF16),
        in_specs=[VMEM],
        out_specs=HBM,
        scratch_shapes=[pltpu.VMEM((size, width), BF16), dma((CHUNKS,))],
        compiler_params=pltpu.CompilerParams(vmem_limit_bytes=16 * 2**20),
        name="swap",
    )(moved)
    return out.reshape(m, rows, width)


def solution(mesh):
    return jax.shard_map(
        body,
        mesh=mesh,
        in_specs=(
            P("mem", "space", None),
            P("space", None),
            P("space", "mem", None),
            P("space", "mem", None),
            P("space", "mem", None),
        ),
        out_specs=P("mem", "space", None),
        check_vma=False,
    )
```

```python
import functools
import math

import jax
import jax.numpy as jnp
from jax import lax
from jax.experimental import pallas as pl
from jax.experimental.pallas import tpu as pltpu
from jax.sharding import PartitionSpec as P

ITERS = 10
PAD = 128
F32 = jnp.float32
BF16 = jnp.bfloat16
MESH = pl.DeviceIdType.MESH
VMEM = pl.BlockSpec(memory_space=pltpu.VMEM)
HBM = pl.BlockSpec(memory_space=pltpu.HBM)
CHUNKS = 4
SPAN = 8


def swap_matrix(outer, inner):
    size = outer * inner
    row = lax.broadcasted_iota(jnp.int32, (size, size), 0)
    column = lax.broadcasted_iota(jnp.int32, (size, size), 1)
    source = (row % inner) * outer + row // inner
    return (source == column).astype(F32).astype(BF16)


def merged(block):
    a, m, c = block.shape
    if m % 16 == 0:
        return block.reshape(a * m, c)
    return block.astype(F32).reshape(a * m, c).astype(BF16)


def halves(value):
    high = value.astype(BF16)
    return high, (value - high.astype(F32)).astype(BF16)


def dot1(a, b):
    return jnp.dot(a, b, preferred_element_type=F32)


def dot3(a, b):
    ah, al = a
    bh, bl = b
    return dot1(ah, bh) + (dot1(ah, bl) + dot1(al, bh))


def step(src, row, diffusion, at, cols):
    lo = PAD + at
    mid = src[row, :, lo : lo + cols]
    around = (
        src[row - 1, :, lo : lo + cols]
        + src[row + 1, :, lo : lo + cols]
        + src[row, :, lo - 1 : lo - 1 + cols]
        + src[row, :, lo + 1 : lo + 1 + cols]
    )
    return mid + diffusion * (around - 4.0 * mid)


def spans(held):
    return [(held[i], held[i : i + SPAN][-1] + 1) for i in range(0, len(held), SPAN)]


def clear_pads(buf, width):
    rows, m, _ = buf.shape
    buf[:, :, :PAD] = jnp.zeros((rows, m, PAD), F32)
    buf[:, :, PAD + width :] = jnp.zeros((rows, m, PAD), F32)


class Peers:
    def __init__(self, n, spaces):
        self.n = n
        self.me = lax.axis_index("mem")
        self.space = lax.axis_index("space")
        self.has_low = self.space > 0
        self.has_high = self.space < spaces - 1
        self.order = []
        for k in range(1, n):
            peer, bit = self.me, 1
            while bit < n:
                if k & bit:
                    peer = peer + bit * (1 - 2 * ((self.me // bit) % 2))
                bit *= 2
            self.order.append(peer)

    def sides(self):
        return ((self.has_low, self.space - 1), (self.has_high, self.space + 1))

    def greet(self):
        barrier = pltpu.get_barrier_semaphore()
        for peer in self.order:
            pl.semaphore_signal(barrier, inc=1, device_id={"mem": peer}, device_id_type=MESH)
        for has, other in self.sides():

            @pl.when(has)
            def _():
                pl.semaphore_signal(barrier, inc=1, device_id={"space": other}, device_id_type=MESH)

    def meet(self):
        barrier = pltpu.get_barrier_semaphore()
        beside = self.has_low.astype(jnp.int32) + self.has_high.astype(jnp.int32)
        pl.semaphore_wait(barrier, self.n - 1 + beside)


class Blocks:
    def __init__(self, peers, src, dst, groups, send, recv):
        self.peers, self.src, self.dst = peers, src, dst
        self.groups, self.sems = groups, (send, recv)

    def copy(self, g, i, slot):
        first, last = self.groups[g]
        peer = self.peers.order[i]
        send, recv = self.sems
        return pltpu.make_async_remote_copy(
            src_ref=self.src.at[peer, first:last],
            dst_ref=self.dst.at[slot, first:last],
            send_sem=send.at[g, i],
            recv_sem=recv.at[g, i],
            device_id={"mem": peer},
            device_id_type=MESH,
        )

    def start(self, g):
        for i in range(len(self.peers.order)):
            self.copy(g, i, self.peers.me).start()
        first, last = self.groups[g]
        me = self.peers.me
        self.dst[me, first:last] = self.src[me, first:last]

    def arrive(self, g, far=True, near=True):
        split = self.peers.n // 2 - 1
        for i in range(0 if near else split, len(self.peers.order) if far else split):
            self.copy(g, i, self.peers.order[i]).wait_recv()

    def finish(self):
        for g in range(len(self.groups)):
            for i in range(len(self.peers.order)):
                self.copy(g, i, self.peers.me).wait_send()


class Rows:
    def __init__(self, peers, src, dst, send, recv):
        self.peers, self.src, self.dst = peers, src, dst
        self.send, self.recv = send, recv

    def copy(self, i, slot):
        peer = self.peers.order[i]
        return pltpu.make_async_remote_copy(
            src_ref=self.src(peer),
            dst_ref=self.dst.at[slot],
            send_sem=self.send.at[i],
            recv_sem=self.recv.at[i],
            device_id={"mem": peer},
            device_id_type=MESH,
        )

    def start(self):
        for i in range(len(self.peers.order)):
            self.copy(i, self.peers.me).start()

    def arrive(self):
        for i in range(len(self.peers.order)):
            self.copy(i, self.peers.order[i]).wait_recv()

    def finish(self):
        for i in range(len(self.peers.order)):
            self.copy(i, self.peers.me).wait_send()


def beside(src, dst, sems, slot, other):
    send, recv = sems
    return pltpu.make_async_remote_copy(
        src_ref=src,
        dst_ref=dst,
        send_sem=send.at[slot],
        recv_sem=recv.at[slot],
        device_id={"space": other},
        device_id_type=MESH,
    )


def cut(first, last, parts):
    size = -(-(last - first) // parts)
    return [(a, min(a + size, last)) for a in range(first, last, size)]


def packed(gram):
    half = gram.shape[0] // 2
    row = lax.broadcasted_iota(jnp.int32, (half, half), 0)
    column = lax.broadcasted_iota(jnp.int32, (half, half), 1)
    last = gram[half:, half:]
    both = jnp.where(row <= column, gram[:half, :half], last)
    diagonal = jnp.sum(jnp.where(row == column, last, 0.0), axis=0, keepdims=True)
    return both, gram[:half, half:], diagonal


def unpacked(both, cross, diagonal):
    half = both.shape[0]
    row = lax.broadcasted_iota(jnp.int32, (half, half), 0)
    column = lax.broadcasted_iota(jnp.int32, (half, half), 1)
    turned = both.T
    first = jnp.where(row <= column, both, turned)
    last = jnp.where(row > column, both, jnp.where(row == column, diagonal, turned))
    top = jnp.concatenate([first, cross], axis=1)
    return jnp.concatenate([top, jnp.concatenate([cross.T, last], axis=1)], axis=0)


def transform_of(gram, vector, members):
    identity = (
        lax.broadcasted_iota(jnp.int32, (members, members), 0)
        == lax.broadcasted_iota(jnp.int32, (members, members), 1)
    ).astype(F32)
    system = gram + (members - 1.0) * identity
    frob = jnp.sqrt(jnp.sum(jnp.sum(system * system, axis=1, keepdims=True), axis=0, keepdims=True))
    root_part = system / frob
    factor = 1.5 * identity - 0.5 * root_part
    root_part = dot3(halves(root_part), halves(factor))
    inverse_part = factor
    for index in range(1, ITERS):
        r, z = halves(root_part), halves(inverse_part)
        f = halves(1.5 * identity - 0.5 * dot3(z, r))
        if index < ITERS - 1:
            root_part = dot3(r, f)
        inverse_part = dot3(f, z)
    inverse_root = inverse_part / jnp.sqrt(frob)
    z = halves(inverse_root)
    weights = dot3(halves(dot3(halves(vector), z)), z)[0:1, :]
    return (math.sqrt(members - 1.0) * inverse_root + weights).astype(BF16)


LEAD, BEFORE = 2, 1


def row_groups(rows):
    middle = rows - 4
    low, high = 4 + middle // 12, 4 + middle // 2
    return [(4, low), (low, high), (0, 4), (high, rows)]


def return_groups(rows):
    return [(0, 4), *cut(4, rows, 3)]


def swap_kernel(moved, out_hbm, out, store):
    rows, m, width = moved.shape
    part = width // CHUNKS
    spans = [pl.ds(c * part, part) for c in range(CHUNKS)]
    stores = [
        pltpu.make_async_copy(out.at[:, span], out_hbm.at[:, span], store.at[c])
        for c, span in enumerate(spans)
    ]
    swap = swap_matrix(m, rows)
    for span, leaving in zip(spans, stores):
        out[:, span] = dot1(swap, merged(moved[:, :, span])).astype(BF16)
        leaving.start()
    for copy in stores:
        copy.wait()


def cycle_kernel(
    spaces, x_hbm, d_hbm, site_hbm, value_hbm, weight_hbm, moved,
    x_ref, d_ref, value_ref, weight_ref, load,
    xs, v1, fresh, patch, updated, back, edge_out, edge_in, d_out, d_in, last_in,
    sites, seen_out, seen, gram_out, gram_in, turned,
    send, recv, return_send, return_recv, side_send, side_recv,
    site_send, site_recv, seen_send, seen_recv, gram_send, gram_recv,
):
    patches, rows, m, cols = patch.shape
    width = patches * cols
    members = patches * m
    obs = value_ref.shape[1]
    peers = Peers(patches, spaces)
    me = peers.me
    part = width // CHUNKS
    loads = [
        pltpu.make_async_copy(
            x_hbm.at[:, c * part : (c + 1) * part], x_ref.at[:, c * part : (c + 1) * part], load.at[c]
        )
        for c in range(CHUNKS)
    ]
    loads += [
        pltpu.make_async_copy(src, dst, load.at[CHUNKS + i])
        for i, (src, dst) in enumerate(
            (
                (d_hbm, d_ref),
                (site_hbm, sites.at[me]),
                (value_hbm, value_ref),
                (weight_hbm, weight_ref),
            )
        )
    ]
    for copy in loads:
        copy.start()
    peers.greet()
    groups = row_groups(rows)
    middle = [group for group in groups if group[0] > 0]
    blocks = Blocks(peers, fresh, patch, groups, send, recv)
    returned = return_groups(rows)
    returns = Blocks(peers, updated, back, returned, return_send, return_recv)
    site_blocks = Rows(peers, lambda peer: sites.at[me], sites, site_send, site_recv)
    seen_blocks = Rows(peers, lambda peer: seen_out.at[peer], seen, seen_send, seen_recv)
    side = (side_send, side_recv)
    sides = list(enumerate(peers.sides()))

    swap = swap_matrix(rows, m)
    clear_pads(xs, width)
    clear_pads(v1, width)
    for at in range(0, width, 2 * cols):
        if at % part == 0:
            loads[at // part].wait()
        turn = dot1(swap, x_ref[:, at : at + 2 * cols]).reshape(rows, m, 2 * cols)
        xs[2 : rows + 2, :, PAD + at : PAD + at + 2 * cols] = turn
        edge_out[0, :, :, at : at + 2 * cols] = turn[:2].astype(BF16)
        edge_out[1, :, :, at : at + 2 * cols] = turn[rows - 2 :].astype(BF16)
    for copy in loads[CHUNKS:]:
        copy.wait()
    d_out[0] = d_ref[0:1, :]
    d_out[1] = d_ref[rows - 1 : rows, :]

    def halo(k, other):
        return (
            beside(edge_out.at[k], edge_in.at[1 - k], side, k, other),
            beside(d_out.at[k], d_in.at[1 - k], side, 2 + k, other),
        )

    def halo_in(k, other):
        return (
            beside(edge_out.at[k], edge_in.at[k], side, 1 - k, other),
            beside(d_out.at[k], d_in.at[k], side, 3 - k, other),
        )

    def first_step(r, d_row):
        for low, high in spans(range(patches)):
            at, to = low * cols, high * cols
            v1[r, :, PAD + at : PAD + to] = step(xs, r, d_row(at, to), at, to - at)

    def second_step(r, place):
        for low, high in spans(range(patches)):
            at, to = low * cols, high * cols
            made = step(v1, r, d_ref[pl.ds(r - 2, 1), at:to], at, to - at).astype(BF16)
            for q in range(low, high):
                fresh[q, place] = made[:, q * cols - at : (q + 1) * cols - at]

    done = 3
    for g, (first, last) in enumerate(middle):

        @pl.loop(done, last + 1)
        def _(r):
            first_step(r, lambda at, to: d_ref[pl.ds(r - 2, 1), at:to])

        done = last + 1

        @pl.loop(first, last)
        def _(r):
            second_step(r, r)

        if g == 0:
            peers.meet()
            for k, (has, other) in sides:

                @pl.when(has)
                def _():
                    for copy in halo(k, other):
                        copy.start()

        if g < LEAD:
            blocks.start(g)
        if g == 0:
            site_blocks.start()

    for k, (has, other) in sides:
        row = 0 if k == 0 else rows + 2

        @pl.when(has)
        def _():
            for copy in halo_in(k, other):
                copy.wait_recv()
            xs[row : row + 2, :, PAD : PAD + width] = edge_in[k].astype(F32)

        @pl.when(jnp.logical_not(has))
        def _():
            xs[row : row + 2, :, PAD : PAD + width] = jnp.zeros((2, m, width), F32)
            d_in[k] = jnp.zeros((1, width), F32)

        outer, inner = (1, 2) if k == 0 else (rows + 2, rows + 1)
        first_step(outer, lambda at, to: d_in[k, :, at:to])
        first_step(inner, lambda at, to: d_ref[inner - 2 : inner - 1, at:to])

        for r in (2, 3) if k == 0 else (rows, rows + 1):
            second_step(r, r % rows)

    site_blocks.arrive()

    @pl.loop(0, patches)
    def _(q):
        lanes = 128
        at = [
            jnp.broadcast_to(sites[q, :, o * lanes : (o + 1) * lanes], (m, lanes))
            for o in range(obs // lanes)
        ]
        lane = [v % lanes for v in at]
        tile = [v // lanes for v in at]
        picked = [jnp.zeros((m, lanes), F32) for _ in at]
        for r in range(rows):
            for h in range(cols // lanes):
                cells = fresh[q, (r + 2) % rows, :, h * lanes : (h + 1) * lanes].astype(F32)
                number = r * (cols // lanes) + h
                for o in range(len(at)):
                    got = jnp.take_along_axis(cells, lane[o], axis=1, mode="promise_in_bounds")
                    picked[o] = jnp.where(tile[o] == number, got, picked[o])
        for o in range(len(at)):
            seen_out[q, :, o * lanes : (o + 1) * lanes] = picked[o].astype(BF16)

    seen_blocks.start()
    seen[me] = seen_out[me]
    for g in range(LEAD, LEAD + BEFORE):
        blocks.start(g)
    seen_blocks.arrive()

    observed = merged(seen[...]).astype(F32)
    obs_mean = jnp.sum(observed, axis=0, keepdims=True) * (1.0 / members)
    root = jnp.sqrt(weight_ref[...])
    spread = ((observed - obs_mean) * root).astype(BF16)
    innovation = ((value_ref[...] - obs_mean) * root).astype(BF16)
    contract = (((1,), (1,)), ((), ()))
    half = members // 2
    both, cross, diagonal = packed(
        lax.dot_general(spread, spread, contract, preferred_element_type=F32)
    )
    gram_out[0, 0:half, 0:half] = both
    gram_out[0, 0:half, half:] = cross
    wide = jnp.broadcast_to(innovation.astype(F32), (8, obs)).astype(BF16)
    gram_out[0, half : half + 8, :] = lax.dot_general(
        wide, spread, contract, preferred_element_type=F32
    )
    gram_out[0, half + 8 :, 0:half] = jnp.broadcast_to(diagonal, (8, half))
    gram_out[0, half + 8 :, half:] = jnp.zeros((8, half), F32)

    def to_beside(stage, k, axis, other):
        return pltpu.make_async_remote_copy(
            src_ref=gram_out.at[stage],
            dst_ref=gram_in.at[stage, 1 - k],
            send_sem=gram_send.at[stage, k],
            recv_sem=gram_recv.at[stage, 1 - k],
            device_id={axis: other},
            device_id_type=MESH,
        )

    def from_beside(stage, k, axis, other):
        return pltpu.make_async_remote_copy(
            src_ref=gram_out.at[stage],
            dst_ref=gram_in.at[stage, k],
            send_sem=gram_send.at[stage, k],
            recv_sem=gram_recv.at[stage, k],
            device_id={axis: other},
            device_id_type=MESH,
        )

    def gram_send_all(stage, axis, pairs):
        for k, (has, other) in enumerate(pairs):

            @pl.when(has)
            def _():
                to_beside(stage, k, axis, other).start()

            @pl.when(jnp.logical_not(has))
            def _():
                gram_in[stage, k] = jnp.zeros((half + 16, members), F32)

    def gram_sum(stage, axis, pairs):
        for k, (has, other) in enumerate(pairs):

            @pl.when(has)
            def _():
                from_beside(stage, k, axis, other).wait_recv()

        return gram_out[stage] + 0.5 * (gram_in[stage, 0] + gram_in[stage, 1])

    along = ((me > 0, me - 1), (me < patches - 1, me + 1))
    gram_send_all(0, "mem", along)
    for g in range(LEAD + BEFORE, len(groups)):
        blocks.start(g)
    gram_out[1] = gram_sum(0, "mem", along)
    gram_send_all(1, "space", peers.sides())
    gram_out[2] = gram_sum(1, "space", peers.sides())
    gram = unpacked(
        gram_out[2, 0:half, 0:half], gram_out[2, 0:half, half:], gram_out[2, half + 8 : half + 9, 0:half]
    )
    turned[...] = transform_of(gram, gram_out[2, half : half + 8], members)

    arrived = set()
    for g, (first, last) in enumerate(returned):
        index = max(i for i, (low, high) in enumerate(groups) if low < last and high > first)
        for earlier in range(index + 1):
            if earlier not in arrived:
                blocks.arrive(earlier)
                arrived.add(earlier)

        @pl.loop(first, last)
        def _(r):
            cells = merged(patch[:, r]).astype(F32)
            mean = jnp.sum(cells, axis=0, keepdims=True) * (1.0 / members)
            result = mean + dot1(turned[...], (cells - mean).astype(BF16))
            updated[:, r] = result.reshape(patches, m, cols).astype(BF16)

        returns.start(g)

    def last_halo(k, other):
        row = 2 if k == 0 else 1
        return beside(back.at[:, row], last_in.at[1 - k], side, 4 + k, other)

    def last_halo_in(k, other):
        return beside(back.at[:, 0], last_in.at[k], side, 5 - k, other)

    def take(r, place, held=range(patches)):
        for q in held:
            xs[r + 1, :, PAD + q * cols : PAD + (q + 1) * cols] = back[q, place].astype(F32)

    def last_step(r, d_row, held=range(patches)):
        for low, high in spans(held):
            at, to = low * cols, high * cols
            moved[r, :, at:to] = step(xs, r + 1, d_row(at, to), at, to - at).astype(BF16)

    returns.arrive(0)
    for k, (has, other) in sides:

        @pl.when(has)
        def _():
            last_halo(k, other).start()

        for r in (0, 1) if k == 0 else (rows - 2, rows - 1):
            take(r, (r + 2) % rows)

    def take_and_step(first, last, done, upto, came, ready):
        @pl.loop(first, last)
        def _(r):
            take(r - 2, r, came)

        @pl.loop(done, upto)
        def _(r):
            last_step(r, lambda at, to: d_ref[pl.ds(r, 1), at:to], ready)

    middle_patch = patches // 2
    done = 1
    for g in range(1, len(returned)):
        first, last = returned[g]
        if g < len(returned) - 1:
            returns.arrive(g)
            take_and_step(first, last, done, last - 3, range(patches), range(patches))
            done = last - 3
        else:
            upper = me >= middle_patch
            returns.arrive(g, far=False)

            @pl.when(upper)
            def _():
                held = range(middle_patch, patches)
                take_and_step(first, last, done, rows - 1, held, held[1:])

            @pl.when(jnp.logical_not(upper))
            def _():
                held = range(middle_patch)
                take_and_step(first, last, done, rows - 1, held, held[:-1])

            returns.arrive(g, near=False)

            @pl.when(upper)
            def _():
                held = range(middle_patch)
                ready = range(middle_patch + 1)
                take_and_step(first, last, done, rows - 1, held, ready)

            @pl.when(jnp.logical_not(upper))
            def _():
                held = range(middle_patch, patches)
                ready = range(middle_patch - 1, patches)
                take_and_step(first, last, done, rows - 1, held, ready)

        if g == 1:
            for k, (has, other) in sides:
                row = 0 if k == 0 else rows + 1

                @pl.when(has)
                def _():
                    last_halo_in(k, other).wait_recv()
                    for q in range(patches):
                        xs[row, :, PAD + q * cols : PAD + (q + 1) * cols] = last_in[k, q].astype(F32)

                @pl.when(jnp.logical_not(has))
                def _():
                    xs[row, :, PAD : PAD + width] = jnp.zeros((m, width), F32)

                r = 0 if k == 0 else rows - 1
                last_step(r, lambda at, to: d_ref[r : r + 1, at:to])

    for sent in (blocks, returns, site_blocks, seen_blocks):
        sent.finish()
    for k, (has, other) in sides:

        @pl.when(has)
        def _():
            for copy in (*halo(k, other), last_halo(k, other)):
                copy.wait_send()

    for stage, axis, pairs in ((0, "mem", along), (1, "space", peers.sides())):
        for k, (has, other) in enumerate(pairs):

            @pl.when(has)
            def _():
                to_beside(stage, k, axis, other).wait_send()


def body(prior, diffusivity, site, quantities, weightings):
    m, rows, width = prior.shape
    patches = lax.axis_size("mem")
    spaces = lax.axis_size("space")
    cols = width // patches
    members = m * patches
    obs = site.shape[-1]
    padded = width + 2 * PAD
    dma = pltpu.SemaphoreType.DMA
    many = len(row_groups(rows))
    others = patches - 1
    args = (
        prior.reshape(m * rows, width),
        diffusivity,
        site[0],
        quantities[0],
        weightings[0],
    )
    bulk = pltpu.VMEM((patches, rows, m, cols), BF16)
    moved = pl.pallas_call(
        functools.partial(cycle_kernel, spaces),
        out_shape=jax.ShapeDtypeStruct((rows, m, width), BF16),
        in_specs=[HBM] * len(args),
        out_specs=VMEM,
        scratch_shapes=[
            pltpu.VMEM((m * rows, width), BF16),
            pltpu.VMEM((rows, width), F32),
            pltpu.VMEM((1, obs), F32),
            pltpu.VMEM((1, obs), F32),
            dma((CHUNKS + 4,)),
            pltpu.VMEM((rows + 4, m, padded), F32),
            pltpu.VMEM((rows + 4, m, padded), F32),
            bulk,
            bulk,
            bulk,
            bulk,
            pltpu.VMEM((2, 2, m, width), BF16),
            pltpu.VMEM((2, 2, m, width), BF16),
            pltpu.VMEM((2, 1, width), F32),
            pltpu.VMEM((2, 1, width), F32),
            pltpu.VMEM((2, patches, m, cols), BF16),
            pltpu.VMEM((patches, 1, obs), jnp.int32),
            pltpu.VMEM((patches, m, obs), BF16),
            pltpu.VMEM((patches, m, obs), BF16),
            pltpu.VMEM((3, members // 2 + 16, members), F32),
            pltpu.VMEM((2, 2, members // 2 + 16, members), F32),
            pltpu.VMEM((members, members), BF16),
            *[dma((many, others))] * 2,
            *[dma((len(return_groups(rows)), others))] * 2,
            dma((6,)),
            dma((6,)),
            *[dma((others,))] * 4,
            dma((2, 2)),
            dma((2, 2)),
        ],
        compiler_params=pltpu.CompilerParams(
            vmem_limit_bytes=44 * 2**20, collective_id=0, has_side_effects=True
        ),
        name="cycle",
    )(*(pltpu.with_memory_space_constraint(arg, pltpu.HBM) for arg in args))
    size = m * rows
    out = pl.pallas_call(
        swap_kernel,
        out_shape=jax.ShapeDtypeStruct((size, width), BF16),
        in_specs=[VMEM],
        out_specs=HBM,
        scratch_shapes=[pltpu.VMEM((size, width), BF16), dma((CHUNKS,))],
        compiler_params=pltpu.CompilerParams(vmem_limit_bytes=16 * 2**20),
        name="swap",
    )(moved)
    return out.reshape(m, rows, width)


def solution(mesh):
    return jax.shard_map(
        body,
        mesh=mesh,
        in_specs=(
            P("mem", "space", None),
            P("space", None),
            P("space", "mem", None),
            P("space", "mem", None),
            P("space", "mem", None),
        ),
        out_specs=P("mem", "space", None),
        check_vma=False,
    )
```

```python
import functools
import math

import jax
import jax.numpy as jnp
from jax import lax
from jax.experimental import pallas as pl
from jax.experimental.pallas import tpu as pltpu
from jax.sharding import PartitionSpec as P

ITERS = 10
PAD = 128
F32 = jnp.float32
BF16 = jnp.bfloat16
MESH = pl.DeviceIdType.MESH
VMEM = pl.BlockSpec(memory_space=pltpu.VMEM)
HBM = pl.BlockSpec(memory_space=pltpu.HBM)
CHUNKS = 4
SPAN = 8


def swap_matrix(outer, inner):
    size = outer * inner
    row = lax.broadcasted_iota(jnp.int32, (size, size), 0)
    column = lax.broadcasted_iota(jnp.int32, (size, size), 1)
    source = (row % inner) * outer + row // inner
    return (source == column).astype(F32).astype(BF16)


def merged(block):
    a, m, c = block.shape
    if m % 16 == 0:
        return block.reshape(a * m, c)
    return block.astype(F32).reshape(a * m, c).astype(BF16)


def halves(value):
    high = value.astype(BF16)
    return high, (value - high.astype(F32)).astype(BF16)


def dot1(a, b):
    return jnp.dot(a, b, preferred_element_type=F32)


def dot3(a, b):
    ah, al = a
    bh, bl = b
    return dot1(ah, bh) + (dot1(ah, bl) + dot1(al, bh))


def step(src, row, diffusion, at, cols):
    lo = PAD + at
    mid = src[row, :, lo : lo + cols]
    around = (
        src[row - 1, :, lo : lo + cols]
        + src[row + 1, :, lo : lo + cols]
        + src[row, :, lo - 1 : lo - 1 + cols]
        + src[row, :, lo + 1 : lo + 1 + cols]
    )
    return mid + diffusion * (around - 4.0 * mid)


def spans(held):
    return [(held[i], held[i : i + SPAN][-1] + 1) for i in range(0, len(held), SPAN)]


def clear_pads(buf, width):
    rows, m, _ = buf.shape
    buf[:, :, :PAD] = jnp.zeros((rows, m, PAD), F32)
    buf[:, :, PAD + width :] = jnp.zeros((rows, m, PAD), F32)


class Peers:
    def __init__(self, n, spaces):
        self.n = n
        self.me = lax.axis_index("mem")
        self.space = lax.axis_index("space")
        self.has_low = self.space > 0
        self.has_high = self.space < spaces - 1
        self.order = []
        for k in range(1, n):
            peer, bit = self.me, 1
            while bit < n:
                if k & bit:
                    peer = peer + bit * (1 - 2 * ((self.me // bit) % 2))
                bit *= 2
            self.order.append(peer)

    def sides(self):
        return ((self.has_low, self.space - 1), (self.has_high, self.space + 1))

    def greet(self):
        barrier = pltpu.get_barrier_semaphore()
        for peer in self.order:
            pl.semaphore_signal(barrier, inc=1, device_id={"mem": peer}, device_id_type=MESH)
        for has, other in self.sides():

            @pl.when(has)
            def _():
                pl.semaphore_signal(barrier, inc=1, device_id={"space": other}, device_id_type=MESH)

    def meet(self):
        barrier = pltpu.get_barrier_semaphore()
        beside = self.has_low.astype(jnp.int32) + self.has_high.astype(jnp.int32)
        pl.semaphore_wait(barrier, self.n - 1 + beside)


class Blocks:
    def __init__(self, peers, src, dst, groups, send, recv):
        self.peers, self.src, self.dst = peers, src, dst
        self.groups, self.sems = groups, (send, recv)

    def copy(self, g, i, slot):
        first, last = self.groups[g]
        peer = self.peers.order[i]
        send, recv = self.sems
        return pltpu.make_async_remote_copy(
            src_ref=self.src.at[peer, first:last],
            dst_ref=self.dst.at[slot, first:last],
            send_sem=send.at[g, i],
            recv_sem=recv.at[g, i],
            device_id={"mem": peer},
            device_id_type=MESH,
        )

    def start(self, g):
        for i in range(len(self.peers.order)):
            self.copy(g, i, self.peers.me).start()
        first, last = self.groups[g]
        me = self.peers.me
        self.dst[me, first:last] = self.src[me, first:last]

    def arrive(self, g, far=True, near=True):
        split = self.peers.n // 2 - 1
        for i in range(0 if near else split, len(self.peers.order) if far else split):
            self.copy(g, i, self.peers.order[i]).wait_recv()

    def finish(self):
        for g in range(len(self.groups)):
            for i in range(len(self.peers.order)):
                self.copy(g, i, self.peers.me).wait_send()


class Rows:
    def __init__(self, peers, src, dst, send, recv):
        self.peers, self.src, self.dst = peers, src, dst
        self.send, self.recv = send, recv

    def copy(self, i, slot):
        peer = self.peers.order[i]
        return pltpu.make_async_remote_copy(
            src_ref=self.src(peer),
            dst_ref=self.dst.at[slot],
            send_sem=self.send.at[i],
            recv_sem=self.recv.at[i],
            device_id={"mem": peer},
            device_id_type=MESH,
        )

    def start(self):
        for i in reversed(range(len(self.peers.order))):
            self.copy(i, self.peers.me).start()

    def arrive(self):
        for i in range(len(self.peers.order)):
            self.copy(i, self.peers.order[i]).wait_recv()

    def finish(self):
        for i in range(len(self.peers.order)):
            self.copy(i, self.peers.me).wait_send()


def beside(src, dst, sems, slot, other):
    send, recv = sems
    return pltpu.make_async_remote_copy(
        src_ref=src,
        dst_ref=dst,
        send_sem=send.at[slot],
        recv_sem=recv.at[slot],
        device_id={"space": other},
        device_id_type=MESH,
    )


def cut(first, last, parts):
    size = -(-(last - first) // parts)
    return [(a, min(a + size, last)) for a in range(first, last, size)]


def packed(gram):
    half = gram.shape[0] // 2
    row = lax.broadcasted_iota(jnp.int32, (half, half), 0)
    column = lax.broadcasted_iota(jnp.int32, (half, half), 1)
    last = gram[half:, half:]
    both = jnp.where(row <= column, gram[:half, :half], last)
    diagonal = jnp.sum(jnp.where(row == column, last, 0.0), axis=0, keepdims=True)
    return both, gram[:half, half:], diagonal


def unpacked(both, cross, diagonal):
    half = both.shape[0]
    row = lax.broadcasted_iota(jnp.int32, (half, half), 0)
    column = lax.broadcasted_iota(jnp.int32, (half, half), 1)
    turned = both.T
    first = jnp.where(row <= column, both, turned)
    last = jnp.where(row > column, both, jnp.where(row == column, diagonal, turned))
    top = jnp.concatenate([first, cross], axis=1)
    return jnp.concatenate([top, jnp.concatenate([cross.T, last], axis=1)], axis=0)


def transform_of(gram, vector, members):
    identity = (
        lax.broadcasted_iota(jnp.int32, (members, members), 0)
        == lax.broadcasted_iota(jnp.int32, (members, members), 1)
    ).astype(F32)
    system = gram + (members - 1.0) * identity
    frob = jnp.sqrt(jnp.sum(jnp.sum(system * system, axis=1, keepdims=True), axis=0, keepdims=True))
    root_part = system / frob
    factor = 1.5 * identity - 0.5 * root_part
    root_part = dot3(halves(root_part), halves(factor))
    inverse_part = factor
    for index in range(1, ITERS):
        r, z = halves(root_part), halves(inverse_part)
        f = halves(1.5 * identity - 0.5 * dot3(z, r))
        if index < ITERS - 1:
            root_part = dot3(r, f)
        inverse_part = dot3(f, z)
    inverse_root = inverse_part / jnp.sqrt(frob)
    z = halves(inverse_root)
    weights = dot3(halves(dot3(halves(vector), z)), z)[0:1, :]
    return (math.sqrt(members - 1.0) * inverse_root + weights).astype(BF16)


LEAD, BEFORE = 2, 1


def row_groups(rows):
    middle = rows - 4
    low, high = 4 + middle // 12, 4 + middle // 2
    return [(4, low), (low, high), (0, 4), (high, rows)]


def return_groups(rows):
    return [(0, 4), *cut(4, rows, 3)]


def swap_kernel(moved, out_hbm, out, store):
    rows, m, width = moved.shape
    part = width // CHUNKS
    spans = [pl.ds(c * part, part) for c in range(CHUNKS)]
    stores = [
        pltpu.make_async_copy(out.at[:, span], out_hbm.at[:, span], store.at[c])
        for c, span in enumerate(spans)
    ]
    swap = swap_matrix(m, rows)
    for span, leaving in zip(spans, stores):
        out[:, span] = dot1(swap, merged(moved[:, :, span])).astype(BF16)
        leaving.start()
    for copy in stores:
        copy.wait()


def cycle_kernel(
    spaces, x_hbm, d_hbm, site_hbm, value_hbm, weight_hbm, moved,
    x_ref, d_ref, value_ref, weight_ref, load,
    xs, v1, fresh, patch, updated, back, edge_out, edge_in, d_out, d_in, last_in,
    sites, seen_out, seen, gram_out, gram_in, turned,
    send, recv, return_send, return_recv, side_send, side_recv,
    site_send, site_recv, seen_send, seen_recv, gram_send, gram_recv,
):
    patches, rows, m, cols = patch.shape
    width = patches * cols
    members = patches * m
    obs = value_ref.shape[1]
    peers = Peers(patches, spaces)
    me = peers.me
    part = width // CHUNKS
    loads = [
        pltpu.make_async_copy(
            x_hbm.at[:, c * part : (c + 1) * part], x_ref.at[:, c * part : (c + 1) * part], load.at[c]
        )
        for c in range(CHUNKS)
    ]
    loads += [
        pltpu.make_async_copy(src, dst, load.at[CHUNKS + i])
        for i, (src, dst) in enumerate(
            (
                (d_hbm, d_ref),
                (site_hbm, sites.at[me]),
                (value_hbm, value_ref),
                (weight_hbm, weight_ref),
            )
        )
    ]
    for copy in loads:
        copy.start()
    peers.greet()
    groups = row_groups(rows)
    middle = [group for group in groups if group[0] > 0]
    blocks = Blocks(peers, fresh, patch, groups, send, recv)
    returned = return_groups(rows)
    returns = Blocks(peers, updated, back, returned, return_send, return_recv)
    site_blocks = Rows(peers, lambda peer: sites.at[me], sites, site_send, site_recv)
    seen_blocks = Rows(peers, lambda peer: seen_out.at[peer], seen, seen_send, seen_recv)
    side = (side_send, side_recv)
    sides = list(enumerate(peers.sides()))

    swap = swap_matrix(rows, m)
    clear_pads(xs, width)
    clear_pads(v1, width)
    for at in range(0, width, 2 * cols):
        if at % part == 0:
            loads[at // part].wait()
        turn = dot1(swap, x_ref[:, at : at + 2 * cols]).reshape(rows, m, 2 * cols)
        xs[2 : rows + 2, :, PAD + at : PAD + at + 2 * cols] = turn
        edge_out[0, :, :, at : at + 2 * cols] = turn[:2].astype(BF16)
        edge_out[1, :, :, at : at + 2 * cols] = turn[rows - 2 :].astype(BF16)
    for copy in loads[CHUNKS:]:
        copy.wait()
    d_out[0] = d_ref[0:1, :]
    d_out[1] = d_ref[rows - 1 : rows, :]

    def halo(k, other):
        return (
            beside(edge_out.at[k], edge_in.at[1 - k], side, k, other),
            beside(d_out.at[k], d_in.at[1 - k], side, 2 + k, other),
        )

    def halo_in(k, other):
        return (
            beside(edge_out.at[k], edge_in.at[k], side, 1 - k, other),
            beside(d_out.at[k], d_in.at[k], side, 3 - k, other),
        )

    def first_step(r, d_row):
        for low, high in spans(range(patches)):
            at, to = low * cols, high * cols
            v1[r, :, PAD + at : PAD + to] = step(xs, r, d_row(at, to), at, to - at)

    def second_step(r, place):
        for low, high in spans(range(patches)):
            at, to = low * cols, high * cols
            made = step(v1, r, d_ref[pl.ds(r - 2, 1), at:to], at, to - at).astype(BF16)
            for q in range(low, high):
                fresh[q, place] = made[:, q * cols - at : (q + 1) * cols - at]

    done = 3
    for g, (first, last) in enumerate(middle):

        @pl.loop(done, last + 1)
        def _(r):
            first_step(r, lambda at, to: d_ref[pl.ds(r - 2, 1), at:to])

        done = last + 1

        @pl.loop(first, last)
        def _(r):
            second_step(r, r)

        if g == 0:
            peers.meet()
            for k, (has, other) in sides:

                @pl.when(has)
                def _():
                    for copy in halo(k, other):
                        copy.start()

        if g < LEAD:
            blocks.start(g)
        if g == 0:
            site_blocks.start()

    for k, (has, other) in sides:
        row = 0 if k == 0 else rows + 2

        @pl.when(has)
        def _():
            for copy in halo_in(k, other):
                copy.wait_recv()
            xs[row : row + 2, :, PAD : PAD + width] = edge_in[k].astype(F32)

        @pl.when(jnp.logical_not(has))
        def _():
            xs[row : row + 2, :, PAD : PAD + width] = jnp.zeros((2, m, width), F32)
            d_in[k] = jnp.zeros((1, width), F32)

        outer, inner = (1, 2) if k == 0 else (rows + 2, rows + 1)
        first_step(outer, lambda at, to: d_in[k, :, at:to])
        first_step(inner, lambda at, to: d_ref[inner - 2 : inner - 1, at:to])

        for r in (2, 3) if k == 0 else (rows, rows + 1):
            second_step(r, r % rows)

    site_blocks.arrive()

    @pl.loop(0, patches)
    def _(q):
        lanes = 128
        at = [
            jnp.broadcast_to(sites[q, :, o * lanes : (o + 1) * lanes], (m, lanes))
            for o in range(obs // lanes)
        ]
        lane = [v % lanes for v in at]
        tile = [v // lanes for v in at]
        picked = [jnp.zeros((m, lanes), F32) for _ in at]
        for r in range(rows):
            for h in range(cols // lanes):
                cells = fresh[q, (r + 2) % rows, :, h * lanes : (h + 1) * lanes].astype(F32)
                number = r * (cols // lanes) + h
                for o in range(len(at)):
                    got = jnp.take_along_axis(cells, lane[o], axis=1, mode="promise_in_bounds")
                    picked[o] = jnp.where(tile[o] == number, got, picked[o])
        for o in range(len(at)):
            seen_out[q, :, o * lanes : (o + 1) * lanes] = picked[o].astype(BF16)

    seen_blocks.start()
    seen[me] = seen_out[me]
    for g in range(LEAD, LEAD + BEFORE):
        blocks.start(g)
    seen_blocks.arrive()

    observed = merged(seen[...]).astype(F32)
    obs_mean = jnp.sum(observed, axis=0, keepdims=True) * (1.0 / members)
    root = jnp.sqrt(weight_ref[...])
    spread = ((observed - obs_mean) * root).astype(BF16)
    innovation = ((value_ref[...] - obs_mean) * root).astype(BF16)
    contract = (((1,), (1,)), ((), ()))
    half = members // 2
    both, cross, diagonal = packed(
        lax.dot_general(spread, spread, contract, preferred_element_type=F32)
    )
    gram_out[0, 0:half, 0:half] = both
    gram_out[0, 0:half, half:] = cross
    wide = jnp.broadcast_to(innovation.astype(F32), (8, obs)).astype(BF16)
    gram_out[0, half : half + 8, :] = lax.dot_general(
        wide, spread, contract, preferred_element_type=F32
    )
    gram_out[0, half + 8 :, 0:half] = jnp.broadcast_to(diagonal, (8, half))
    gram_out[0, half + 8 :, half:] = jnp.zeros((8, half), F32)

    def to_beside(stage, k, axis, other):
        return pltpu.make_async_remote_copy(
            src_ref=gram_out.at[stage],
            dst_ref=gram_in.at[stage, 1 - k],
            send_sem=gram_send.at[stage, k],
            recv_sem=gram_recv.at[stage, 1 - k],
            device_id={axis: other},
            device_id_type=MESH,
        )

    def from_beside(stage, k, axis, other):
        return pltpu.make_async_remote_copy(
            src_ref=gram_out.at[stage],
            dst_ref=gram_in.at[stage, k],
            send_sem=gram_send.at[stage, k],
            recv_sem=gram_recv.at[stage, k],
            device_id={axis: other},
            device_id_type=MESH,
        )

    def gram_send_all(stage, axis, pairs):
        for k, (has, other) in enumerate(pairs):

            @pl.when(has)
            def _():
                to_beside(stage, k, axis, other).start()

            @pl.when(jnp.logical_not(has))
            def _():
                gram_in[stage, k] = jnp.zeros((half + 16, members), F32)

    def gram_sum(stage, axis, pairs):
        for k, (has, other) in enumerate(pairs):

            @pl.when(has)
            def _():
                from_beside(stage, k, axis, other).wait_recv()

        return gram_out[stage] + 0.5 * (gram_in[stage, 0] + gram_in[stage, 1])

    along = ((me > 0, me - 1), (me < patches - 1, me + 1))
    gram_send_all(0, "mem", along)
    for g in range(LEAD + BEFORE, len(groups)):
        blocks.start(g)
    gram_out[1] = gram_sum(0, "mem", along)
    gram_send_all(1, "space", peers.sides())
    gram_out[2] = gram_sum(1, "space", peers.sides())
    gram = unpacked(
        gram_out[2, 0:half, 0:half], gram_out[2, 0:half, half:], gram_out[2, half + 8 : half + 9, 0:half]
    )
    turned[...] = transform_of(gram, gram_out[2, half : half + 8], members)

    arrived = set()
    for g, (first, last) in enumerate(returned):
        index = max(i for i, (low, high) in enumerate(groups) if low < last and high > first)
        for earlier in range(index + 1):
            if earlier not in arrived:
                blocks.arrive(earlier)
                arrived.add(earlier)

        @pl.loop(first, last)
        def _(r):
            cells = merged(patch[:, r]).astype(F32)
            mean = jnp.sum(cells, axis=0, keepdims=True) * (1.0 / members)
            result = mean + dot1(turned[...], (cells - mean).astype(BF16))
            updated[:, r] = result.reshape(patches, m, cols).astype(BF16)

        returns.start(g)

    def last_halo(k, other):
        row = 2 if k == 0 else 1
        return beside(back.at[:, row], last_in.at[1 - k], side, 4 + k, other)

    def last_halo_in(k, other):
        return beside(back.at[:, 0], last_in.at[k], side, 5 - k, other)

    def take(r, place, held=range(patches)):
        for q in held:
            xs[r + 1, :, PAD + q * cols : PAD + (q + 1) * cols] = back[q, place].astype(F32)

    def last_step(r, d_row, held=range(patches)):
        for low, high in spans(held):
            at, to = low * cols, high * cols
            moved[r, :, at:to] = step(xs, r + 1, d_row(at, to), at, to - at).astype(BF16)

    returns.arrive(0)
    for k, (has, other) in sides:

        @pl.when(has)
        def _():
            last_halo(k, other).start()

        for r in (0, 1) if k == 0 else (rows - 2, rows - 1):
            take(r, (r + 2) % rows)

    def take_and_step(first, last, done, upto, came, ready):
        @pl.loop(first, last)
        def _(r):
            take(r - 2, r, came)

        @pl.loop(done, upto)
        def _(r):
            last_step(r, lambda at, to: d_ref[pl.ds(r, 1), at:to], ready)

    middle_patch = patches // 2
    done = 1
    for g in range(1, len(returned)):
        first, last = returned[g]
        if g < len(returned) - 1:
            returns.arrive(g)
            take_and_step(first, last, done, last - 3, range(patches), range(patches))
            done = last - 3
        else:
            upper = me >= middle_patch
            returns.arrive(g, far=False)

            @pl.when(upper)
            def _():
                held = range(middle_patch, patches)
                take_and_step(first, last, done, rows - 1, held, held[1:])

            @pl.when(jnp.logical_not(upper))
            def _():
                held = range(middle_patch)
                take_and_step(first, last, done, rows - 1, held, held[:-1])

            returns.arrive(g, near=False)

            @pl.when(upper)
            def _():
                held = range(middle_patch)
                ready = range(middle_patch + 1)
                take_and_step(first, last, done, rows - 1, held, ready)

            @pl.when(jnp.logical_not(upper))
            def _():
                held = range(middle_patch, patches)
                ready = range(middle_patch - 1, patches)
                take_and_step(first, last, done, rows - 1, held, ready)

        if g == 1:
            for k, (has, other) in sides:
                row = 0 if k == 0 else rows + 1

                @pl.when(has)
                def _():
                    last_halo_in(k, other).wait_recv()
                    for q in range(patches):
                        xs[row, :, PAD + q * cols : PAD + (q + 1) * cols] = last_in[k, q].astype(F32)

                @pl.when(jnp.logical_not(has))
                def _():
                    xs[row, :, PAD : PAD + width] = jnp.zeros((m, width), F32)

                r = 0 if k == 0 else rows - 1
                last_step(r, lambda at, to: d_ref[r : r + 1, at:to])

    for sent in (blocks, returns, site_blocks, seen_blocks):
        sent.finish()
    for k, (has, other) in sides:

        @pl.when(has)
        def _():
            for copy in (*halo(k, other), last_halo(k, other)):
                copy.wait_send()

    for stage, axis, pairs in ((0, "mem", along), (1, "space", peers.sides())):
        for k, (has, other) in enumerate(pairs):

            @pl.when(has)
            def _():
                to_beside(stage, k, axis, other).wait_send()


def body(prior, diffusivity, site, quantities, weightings):
    m, rows, width = prior.shape
    patches = lax.axis_size("mem")
    spaces = lax.axis_size("space")
    cols = width // patches
    members = m * patches
    obs = site.shape[-1]
    padded = width + 2 * PAD
    dma = pltpu.SemaphoreType.DMA
    many = len(row_groups(rows))
    others = patches - 1
    args = (
        prior.reshape(m * rows, width),
        diffusivity,
        site[0],
        quantities[0],
        weightings[0],
    )
    bulk = pltpu.VMEM((patches, rows, m, cols), BF16)
    moved = pl.pallas_call(
        functools.partial(cycle_kernel, spaces),
        out_shape=jax.ShapeDtypeStruct((rows, m, width), BF16),
        in_specs=[HBM] * len(args),
        out_specs=VMEM,
        scratch_shapes=[
            pltpu.VMEM((m * rows, width), BF16),
            pltpu.VMEM((rows, width), F32),
            pltpu.VMEM((1, obs), F32),
            pltpu.VMEM((1, obs), F32),
            dma((CHUNKS + 4,)),
            pltpu.VMEM((rows + 4, m, padded), F32),
            pltpu.VMEM((rows + 4, m, padded), F32),
            bulk,
            bulk,
            bulk,
            bulk,
            pltpu.VMEM((2, 2, m, width), BF16),
            pltpu.VMEM((2, 2, m, width), BF16),
            pltpu.VMEM((2, 1, width), F32),
            pltpu.VMEM((2, 1, width), F32),
            pltpu.VMEM((2, patches, m, cols), BF16),
            pltpu.VMEM((patches, 1, obs), jnp.int32),
            pltpu.VMEM((patches, m, obs), BF16),
            pltpu.VMEM((patches, m, obs), BF16),
            pltpu.VMEM((3, members // 2 + 16, members), F32),
            pltpu.VMEM((2, 2, members // 2 + 16, members), F32),
            pltpu.VMEM((members, members), BF16),
            *[dma((many, others))] * 2,
            *[dma((len(return_groups(rows)), others))] * 2,
            dma((6,)),
            dma((6,)),
            *[dma((others,))] * 4,
            dma((2, 2)),
            dma((2, 2)),
        ],
        compiler_params=pltpu.CompilerParams(
            vmem_limit_bytes=44 * 2**20, collective_id=0, has_side_effects=True
        ),
        name="cycle",
    )(*(pltpu.with_memory_space_constraint(arg, pltpu.HBM) for arg in args))
    size = m * rows
    out = pl.pallas_call(
        swap_kernel,
        out_shape=jax.ShapeDtypeStruct((size, width), BF16),
        in_specs=[VMEM],
        out_specs=HBM,
        scratch_shapes=[pltpu.VMEM((size, width), BF16), dma((CHUNKS,))],
        compiler_params=pltpu.CompilerParams(vmem_limit_bytes=16 * 2**20),
        name="swap",
    )(moved)
    return out.reshape(m, rows, width)


def solution(mesh):
    return jax.shard_map(
        body,
        mesh=mesh,
        in_specs=(
            P("mem", "space", None),
            P("space", None),
            P("space", "mem", None),
            P("space", "mem", None),
            P("space", "mem", None),
        ),
        out_specs=P("mem", "space", None),
        check_vma=False,
    )
```
